256 devices in a mesh: tm: 16 (over y_hi, z), sub: 16 (over x, y_lo, core).
Axes of the slice: x: 4, y: 4 (y_hi: 2, y_lo: 2; y = y_hi * 2 + y_lo), z: 8, core: 2. Of those that a mesh axis runs over, the one named last changes fastest.
Arguments:
- frames: bfloat16 [16384, 1024], P(('tm', 'sub')), may hold values from -16 to 16
- modulation: float32 [8, 1024], replicated, may hold values from -4 to 4
- w_project: bfloat16 [3, 1024, 1024], P(None, None, 'sub'), may hold values from -1 to 1
- w_heads_out: bfloat16 [1024, 1024], P('sub'), may hold values from -0.25 to 0.25
- w_up: bfloat16 [1024, 4096], P(None, 'sub'), may hold values from -0.1875 to 0.1875
- w_down: bfloat16 [4096, 1024], P('sub'), may hold values from -0.125 to 0.125
- w_velocity: bfloat16 [1024, 100], replicated, may hold values from -0.1875 to 0.1875
- noisy_mel: float32 [16384, 100], P('tm'), may hold values from -6 to 6
- w_prelude: bfloat16 [7, 1536, 100], P(None, 'sub'), may hold values from -0.21875 to 0.21875
- w_upsample: bfloat16 [8, 1536, 768], P(None, 'sub'), may hold values from -0.109375 to 0.109375
- snake_alpha: float32 [2, 768], replicated, may hold values from 0.3 to 3
- w_dilated: bfloat16 [3, 768, 768], P(None, 'sub'), may hold values from -0.125 to 0.125
- w_plain: bfloat16 [3, 768, 768], P(None, 'sub'), may hold values from -0.125 to 0.125
Outputs:
- mel_next: float32 [16384, 100], P('tm')
- section_out: bfloat16 [65536, 768], P(('tm', 'sub'))
The draws below stay inside these ranges and needn't reach their ends.
All inputs are finite; a program needn't handle non-finite values.
Results may differ from the reference program's by a relative error of at most 0.03.
Values may be sent and summed in bfloat16 or wider, within the bound.
No kernel may reach another device: no remote copies, remote signals or barrier semaphores. Data moves between devices by JAX's collectives and lax.ppermute only.
A program may use at most 64 MiB of HBM per device.

```python
import math
import jax
import jax.numpy as jnp
from jax import lax

D = 1024
HEADS = 16
HEAD_DIM = 64
FF = 4096
MEL = 100
C_IN = 1536
C_MID = 768
BLK = 256
FRAMES = 16384
N_SUB = 16


def draw_frames(key, part):
    own_key = jax.random.fold_in(key, 11)
    entries = jax.random.normal(jax.random.fold_in(own_key, 1), (FRAMES, D), jnp.float32)
    drawn = entries
    return jnp.clip(drawn, -16.0, 16.0).astype(jnp.bfloat16)


def draw_w_project(key, part):
    own_key = jax.random.fold_in(key, 12)
    drawn = jnp.clip(jax.random.normal(jax.random.fold_in(own_key, 2), (3, D, D), jnp.float32), -6.0, 6.0) / math.sqrt(D)
    return jnp.clip(drawn, -1.0, 1.0).astype(jnp.bfloat16)


def strengthened(values, stream_key, source, target, shards_of, factor):
    owner, partner = [(jnp.arange(values.shape[axis_at]) // (values.shape[axis_at] // shards_of)).reshape([-1 if axis == axis_at else 1 for axis in range(values.ndim)]) for axis_at in (source, target)]
    chosen = jax.random.permutation(stream_key, shards_of)[partner]
    strong = (owner == chosen) | (owner == (partner + shards_of // 2) % shards_of)
    return jnp.where(strong, factor * values, values)


def shard_levels(key, dims, pieces, low, top_value):
    gain, own = 1.0, jax.random.fold_in(key, 6)
    for axis_at, shards_of in pieces:
        heights = jnp.exp(jax.random.uniform(jax.random.fold_in(own, axis_at), (shards_of,), jnp.float32, low / len(pieces), top_value / len(pieces)))
        gain = gain * jnp.repeat(heights, dims[axis_at] // shards_of).reshape([-1 if axis == axis_at else 1 for axis in range(len(dims))])
    return gain


def gaussian(stream_key, dims, scale, reach, shards=(), held_as=jnp.bfloat16):
    factor_of = shard_levels(stream_key, dims, shards, -0.22, 0.18) if shards else 1.0
    values = jax.random.normal(stream_key, dims, jnp.float32) * scale * factor_of
    return jnp.minimum(jnp.maximum(values, -reach), reach).astype(held_as)


def noise_with(rng, shape, width, reach, split, heavy, held_as=jnp.bfloat16):
    values = width * jax.random.normal(rng, shape, jnp.float32)
    if split:
        values = values * shard_levels(rng, shape, split, -0.22, 0.18)
    return jnp.clip(strengthened(values, jax.random.fold_in(rng, 3), *heavy), -reach, reach).astype(held_as)


def setup_inputs(seed: int = 0) -> dict:
    streams_of = jax.random.split(jax.random.key(seed), 14)
    return {
        "frames": draw_frames(jax.random.fold_in(streams_of[13], 71), 0),
        "modulation": gaussian(streams_of[1], (8, D), 1.0, 4.0, (), jnp.float32),
        "w_project": draw_w_project(jax.random.fold_in(streams_of[13], 71), 0),
        "w_heads_out": noise_with(streams_of[3], (D, D), D ** -0.5, 0.25, ((0, 16),), (0, 1, 16, 2.0)),
        "w_up": gaussian(streams_of[4], (D, FF), D ** -0.5, 0.1875, ((1, 16),)),
        "w_down": noise_with(streams_of[5], (FF, D), FF ** -0.5, 0.125, ((0, 16),), (0, 1, 16, 2.0)),
        "w_velocity": gaussian(streams_of[6], (D, MEL), D ** -0.5, 0.1875),
        "noisy_mel": gaussian(streams_of[7], (FRAMES, MEL), 1.0, 6.0, ((0, 16),), jnp.float32),
        "w_prelude": gaussian(streams_of[8], (7, C_IN, MEL), (7 * MEL) ** -0.5, 0.21875, ((1, 16),)),
        "w_upsample": gaussian(streams_of[9], (8, C_IN, C_MID), (2 * C_IN) ** -0.5, 0.109375, ((1, 16),)),
        "snake_alpha": jnp.clip(jnp.exp(jax.random.uniform(streams_of[10], (2, C_MID), jnp.float32, math.log(0.3), math.log(3.0))), 0.3, 3.0),
        "w_dilated": gaussian(streams_of[11], (3, C_MID, C_MID), (3 * C_MID) ** -0.5, 0.125, ((1, 16),)),
        "w_plain": gaussian(streams_of[12], (3, C_MID, C_MID), (3 * C_MID) ** -0.5, 0.125, ((1, 16),)),
    }


epsilon = 1e-06

def norm_rows(rows, offset_row, scale_row):
    rows = rows.astype(jnp.float32)
    center = lax.optimization_barrier(jnp.mean(rows, axis=-1, keepdims=True))
    square = lax.optimization_barrier(jnp.mean(rows * rows, axis=-1, keepdims=True))
    spread = square - center * center
    return (rows - center) * lax.rsqrt(spread + epsilon) * (1.0 + scale_row) + offset_row

def snake_act(values, alpha_row):
    return values + jnp.square(jnp.sin(alpha_row * values)) / alpha_row

def settle(values):
    return lax.optimization_barrier(values.astype(jnp.bfloat16)).astype(jnp.float32)

def grouped_product(left, right, groups):
    group_width = left.shape[1] // groups

    def add_group(group_index, running):
        first_col = (group_index * group_width).astype(jnp.int32)
        part_left = lax.dynamic_slice_in_dim(left, first_col, group_width, 1)
        part_right = lax.dynamic_slice_in_dim(right, first_col, group_width, 0)
        return running + settle(jnp.dot(part_left, part_right, preferred_element_type=jnp.float32))
    empty_sum = jnp.zeros((left.shape[0], right.shape[1]), jnp.float32)
    return lax.fori_loop(0, groups, add_group, empty_sum)

def block_attention(queries, keys_now, values_now):
    blocks = FRAMES // BLK
    block_shape = (blocks, BLK, HEADS, HEAD_DIM)
    query_blocks = queries.reshape(block_shape)
    key_blocks = keys_now.reshape(block_shape)
    value_blocks = values_now.reshape(block_shape)
    empty_block = jnp.zeros((1, BLK, HEADS, HEAD_DIM), jnp.bfloat16)
    key_all = jnp.concatenate([jnp.concatenate([empty_block, key_blocks[:-1]], 0), key_blocks], 1)
    value_all = jnp.concatenate([jnp.concatenate([empty_block, value_blocks[:-1]], 0), value_blocks], 1)
    leading = jnp.arange(blocks) == 0

    def one_block(inputs):
        query_one, key_one, value_one, is_lead = inputs
        scores = jnp.einsum('qhd,khd->hqk', query_one.astype(jnp.float32), key_one.astype(jnp.float32)) / math.sqrt(HEAD_DIM)
        allowed = jnp.logical_or(jnp.logical_not(is_lead), jnp.arange(2 * BLK) >= BLK)
        scores = jnp.where(allowed[None, None, :], scores, -1e+30)
        largest = lax.optimization_barrier(jnp.max(scores, axis=-1, keepdims=True))
        raised = jnp.exp(scores - largest)
        weights = (raised / lax.optimization_barrier(jnp.sum(raised, axis=-1, keepdims=True))).astype(jnp.bfloat16)
        attended = jnp.einsum('hqk,khd->qhd', weights.astype(jnp.float32), value_one.astype(jnp.float32))
        return attended.astype(jnp.bfloat16)
    attended = lax.map(one_block, (query_blocks, key_all, value_all, leading))
    return attended.reshape((FRAMES, D))

def upsample(prelude, w_upsample):
    group_width = C_IN // N_SUB
    padded = jnp.pad(prelude, ((1, 1), (0, 0)))

    def add_group(group_index, running):
        first_col = (group_index * group_width).astype(jnp.int32)
        part_left = lax.dynamic_slice_in_dim(padded, first_col, group_width, 1)
        tap_weights = lax.dynamic_slice_in_dim(w_upsample, first_col, group_width, 1)
        current = part_left[1:-1]
        earlier = part_left[:-2]
        later_frames = part_left[2:]

        def tap_product(source, offset):
            return jnp.dot(source, tap_weights[offset], preferred_element_type=jnp.float32)
        phases = jnp.stack([tap_product(current, 2) + tap_product(earlier, 6), tap_product(current, 3) + tap_product(earlier, 7), tap_product(current, 4) + tap_product(later_frames, 0), tap_product(current, 5) + tap_product(later_frames, 1)], 1)
        return running + settle(phases.reshape((4 * FRAMES, C_MID)))
    empty_sum = jnp.zeros((4 * FRAMES, C_MID), jnp.float32)
    return lax.fori_loop(0, N_SUB, add_group, empty_sum).astype(jnp.bfloat16)

def kernel_conv(source, weight, gap):
    length = source.shape[0]
    padded = jnp.pad(source, ((gap, gap), (0, 0)))
    running = jnp.zeros((length, weight.shape[2]), jnp.float32)
    for offset in range(3):
        running = running + jnp.dot(padded[offset * gap:offset * gap + length], weight[offset], preferred_element_type=jnp.float32)
    return running

def reference(frames, modulation, w_project, w_heads_out, w_up, w_down, w_velocity, noisy_mel, w_prelude, w_upsample, snake_alpha, w_dilated, w_plain):
    first_norm = norm_rows(frames, modulation[0], modulation[1]).astype(jnp.bfloat16)
    queries = jnp.dot(first_norm, w_project[0], preferred_element_type=jnp.float32).astype(jnp.bfloat16)
    keys_now = jnp.dot(first_norm, w_project[1], preferred_element_type=jnp.float32).astype(jnp.bfloat16)
    values_now = jnp.dot(first_norm, w_project[2], preferred_element_type=jnp.float32).astype(jnp.bfloat16)
    heads_out = block_attention(queries, keys_now, values_now)
    attn = grouped_product(heads_out, w_heads_out, N_SUB)
    mixed_rows = (frames.astype(jnp.float32) + modulation[2] * attn).astype(jnp.bfloat16)
    second_norm = norm_rows(mixed_rows, modulation[3], modulation[4]).astype(jnp.bfloat16)
    hidden = jax.nn.gelu(jnp.dot(second_norm, w_up, preferred_element_type=jnp.float32), approximate=True).astype(jnp.bfloat16)
    feed = grouped_product(hidden, w_down, N_SUB)
    final_rows = (mixed_rows.astype(jnp.float32) + modulation[5] * feed).astype(jnp.bfloat16)
    final_norm = norm_rows(final_rows, modulation[6], modulation[7]).astype(jnp.bfloat16)
    velocity = jnp.dot(final_norm, w_velocity, preferred_element_type=jnp.float32)
    mel_next = noisy_mel + 0.5 * velocity
    mel_low = mel_next.astype(jnp.bfloat16)
    padded = jnp.pad(mel_low, ((3, 3), (0, 0)))
    prelude = jnp.zeros((FRAMES, C_IN), jnp.float32)
    for offset in range(7):
        prelude = prelude + jnp.dot(padded[offset:offset + FRAMES], w_prelude[offset].T, preferred_element_type=jnp.float32)
    prelude = prelude.astype(jnp.bfloat16)
    up_x = upsample(prelude, w_upsample)
    act_one = snake_act(up_x.astype(jnp.float32), snake_alpha[0]).astype(jnp.bfloat16)
    inner_conv = kernel_conv(act_one, w_dilated, 3)
    act_two = snake_act(inner_conv, snake_alpha[1]).astype(jnp.bfloat16)
    outer_conv = kernel_conv(act_two, w_plain, 1)
    section_out = (up_x.astype(jnp.float32) + outer_conv).astype(jnp.bfloat16)
    return (mel_next, section_out)
```

```python
import math

import jax
import jax.numpy as jnp
from jax import lax
from jax.experimental import pallas as pl
from jax.experimental.pallas import tpu as pltpu
from jax.sharding import PartitionSpec as P

HEAD_DIM = 64
BLK = 256
MEL_PAD = 128
OFFSETS = 9
HALO = 8

epsilon = 1e-06
bf16 = jnp.bfloat16
f32 = jnp.float32

X_GROUPS = [[4 * x + j for x in range(4)] for j in range(4)]
J_GROUPS = [[4 * x + j for j in range(4)] for x in range(4)]


def norm_rows(rows, offset_row, scale_row):
    rows = rows.astype(f32)
    center = jnp.mean(rows, axis=-1, keepdims=True)
    square = jnp.mean(rows * rows, axis=-1, keepdims=True)
    spread = square - center * center
    return (rows - center) * lax.rsqrt(spread + epsilon) * (1.0 + scale_row) + offset_row


def mm(a, b):
    return jnp.dot(a, b, preferred_element_type=f32)


def mm_t(a, b):
    return lax.dot_general(a, b, (((1,), (1,)), ((), ())), preferred_element_type=f32)


def vmem_specs(n):
    return [pl.BlockSpec(memory_space=pltpu.VMEM)] * n


def attention_kernel(flag_ref, own_ref, back_ref, w_ref, out_ref, heads, w_out):
    first = flag_ref[0] > 0
    for h in range(4):
        c = 256 * h
        k = own_ref[:, c : c + 64]
        v = own_ref[:, c + 64 : c + 128]
        q = own_ref[:, c + 128 : c + 192]
        kb = back_ref[:, 128 * h : 128 * h + 64]
        vb = back_ref[:, 128 * h + 64 : 128 * h + 128]
        scale = 1.0 / math.sqrt(HEAD_DIM)
        s_own = mm_t(q, k) * scale
        s_back = mm_t(q, kb) * scale
        s_back = jnp.where(first, -1e30, s_back)
        top = jnp.maximum(
            jnp.max(s_own, axis=-1, keepdims=True), jnp.max(s_back, axis=-1, keepdims=True)
        )
        e_own = jnp.exp(s_own - top)
        e_back = jnp.exp(s_back - top)
        total = jnp.sum(e_own, axis=-1, keepdims=True) + jnp.sum(e_back, axis=-1, keepdims=True)
        inv = 1.0 / total
        p_own = (e_own * inv).astype(bf16)
        p_back = (e_back * inv).astype(bf16)
        heads[:, 64 * h : 64 * h + 64] = (mm(p_own, v) + mm(p_back, vb)).astype(bf16)
        w_out[64 * h : 64 * h + 64, :] = w_ref[c + 192 : c + 256, :]
    out_ref[...] = mm(heads[...], w_out[...]).astype(bf16)


def attention(flag, own, back, weights):
    return pl.pallas_call(
        attention_kernel,
        out_shape=jax.ShapeDtypeStruct((BLK, 1024), bf16),
        in_specs=[pl.BlockSpec(memory_space=pltpu.SMEM)] + vmem_specs(3),
        out_specs=pl.BlockSpec(memory_space=pltpu.VMEM),
        scratch_shapes=[pltpu.VMEM((BLK, 256), bf16), pltpu.VMEM((256, 1024), bf16)],
        compiler_params=pltpu.CompilerParams(vmem_limit_bytes=24 << 20),
        cost_estimate=pl.CostEstimate(
            flops=5 * 10**8, bytes_accessed=3 << 20, transcendentals=1 << 19
        ),
        name="attention",
    )(flag, own, back, weights)


def mlp_kernel(h_ref, w0, w1, w2, w3, out_ref, acc):
    h = h_ref[...]
    for i, w in enumerate((w0, w1, w2, w3)):
        up = mm(h, w[0:1024, :])
        hid = jax.nn.gelu(up, approximate=True).astype(bf16)
        for k in range(4):
            part = mm(hid, w[1024 + 256 * k : 1280 + 256 * k, :])
            cols = slice(256 * k, 256 * k + 256)
            if i == 0:
                acc[:, cols] = part
            elif i < 3:
                acc[:, cols] += part
            else:
                out_ref[:, cols] = (acc[:, cols] + part).astype(bf16)


def mlp(h, weights):
    return pl.pallas_call(
        mlp_kernel,
        out_shape=jax.ShapeDtypeStruct((256, 1024), bf16),
        in_specs=vmem_specs(5),
        out_specs=pl.BlockSpec(memory_space=pltpu.VMEM),
        scratch_shapes=[pltpu.VMEM((256, 1024), f32)],
        compiler_params=pltpu.CompilerParams(vmem_limit_bytes=24 << 20),
        cost_estimate=pl.CostEstimate(
            flops=11 * 10**8, bytes_accessed=5 << 20, transcendentals=1 << 18
        ),
        name="mlp",
    )(h, *weights)


def snake_act(values, alpha_row):
    return values + jnp.square(jnp.sin(alpha_row * values)) / alpha_row


def shifted(plane, by):
    return pltpu.roll(plane, by % plane.shape[0], 0)


ROWS = 72


def conv_kernel(flag_ref, up_ref, alpha_ref, w_hbm, out_ref, wa, wb, planes, sem):
    copies = []
    for which, (buf, base) in enumerate(((wa, 96), (wb, 240))):
        mine = []
        for s in range(16):
            for tap in range(3):
                mine.append(
                    pltpu.make_async_copy(
                        w_hbm.at[s, pl.ds(base + 48 * tap, 48), :],
                        buf.at[tap, pl.ds(48 * s, 48), :],
                        sem.at[which],
                    )
                )
        copies.append(mine)
    for mine in copies:
        for c in mine:
            c.start()
    first = flag_ref[0] > 0
    last = flag_ref[1] > 0
    row = lax.broadcasted_iota(jnp.int32, (ROWS, 768), 0)
    outside = (first & (row == 0)) | (last & (row == 65))
    for s in range(16):
        block = up_ref[s]
        for p in range(4):
            planes[p, :, 48 * s : 48 * s + 48] = block[:, 48 * p : 48 * p + 48]
    a1 = alpha_ref[0:1, :]
    a2 = alpha_ref[1:2, :]
    ups = []
    acts = []
    for p in range(4):
        u = jnp.where(outside, 0.0, planes[p].astype(f32))
        ups.append(u)
        acts.append(snake_act(u, a1).astype(bf16))
    act = jnp.concatenate(acts, axis=0)
    for c in copies[0]:
        c.wait()
    y = [mm(act, wa[tap]) for tap in range(3)]
    y = [[v[ROWS * p : ROWS * p + ROWS] for p in range(4)] for v in y]
    acts = []
    for p in range(4):
        before = y[0][0] if p == 3 else shifted(y[0][p + 1], 1)
        after = y[2][3] if p == 0 else shifted(y[2][p - 1], -1)
        inner = before + y[1][p] + after
        acts.append(jnp.where(outside, 0.0, snake_act(inner, a2)).astype(bf16))
    act = jnp.concatenate(acts, axis=0)
    for c in copies[1]:
        c.wait()
    y = [mm(act, wb[tap]) for tap in range(3)]
    y = [[v[ROWS * p : ROWS * p + ROWS] for p in range(4)] for v in y]
    for p in range(4):
        before = y[0][p - 1] if p >= 1 else shifted(y[0][3], 1)
        after = y[2][p + 1] if p <= 2 else shifted(y[2][0], -1)
        total = ups[p] + (before + y[1][p] + after)
        out_ref[:, 768 * p : 768 * p + 768] = shifted(total, -1)[0:64].astype(bf16)


def convolutions(flags, up, alpha, weights):
    return pl.pallas_call(
        conv_kernel,
        out_shape=jax.ShapeDtypeStruct((64, 3072), bf16),
        in_specs=[pl.BlockSpec(memory_space=pltpu.SMEM)]
        + vmem_specs(2)
        + [pl.BlockSpec(memory_space=pl.ANY)],
        out_specs=pl.BlockSpec(memory_space=pltpu.VMEM),
        scratch_shapes=[
            pltpu.VMEM((3, 768, 768), bf16),
            pltpu.VMEM((3, 768, 768), bf16),
            pltpu.VMEM((4, ROWS, 768), bf16),
            pltpu.SemaphoreType.DMA((2,)),
        ],
        compiler_params=pltpu.CompilerParams(vmem_limit_bytes=40 << 20),
        cost_estimate=pl.CostEstimate(
            flops=2 * 10**9, bytes_accessed=8 << 20, transcendentals=1 << 19
        ),
        name="convolutions",
    )(flags, up, alpha, weights)


def body(
    frames,
    modulation,
    w_project,
    w_heads_out,
    w_up,
    w_down,
    w_velocity,
    noisy_mel,
    w_prelude,
    w_upsample,
    snake_alpha,
    w_dilated,
    w_plain,
):
    own_rows = frames.shape[0]
    sub_index = lax.axis_index("sub")
    time_index = lax.axis_index("tm")
    n_sub = lax.axis_size("sub")
    n_tm = lax.axis_size("tm")
    n_all = n_sub * n_tm
    both = ("tm", "sub")

    w_t = jnp.swapaxes(w_project, 1, 2)
    w_att = jnp.concatenate([w_t[1], w_t[2], w_t[0], w_heads_out], axis=0)
    w_att = lax.all_gather(w_att, "sub", axis=0, tiled=True, axis_index_groups=X_GROUPS)

    pre = jnp.transpose(w_prelude, (1, 0, 2)).reshape(96, 700)
    pre = jnp.pad(pre, ((0, 0), (0, 68)))
    w_voc = jnp.concatenate([pre, w_dilated.reshape(144, 768), w_plain.reshape(144, 768)], axis=0)
    w_voc, _ = lax.optimization_barrier((w_voc, w_att))
    w_voc = lax.all_gather(w_voc, "sub", axis=0, tiled=False)

    own_w = jnp.concatenate([w_up] + [w_down[:, 256 * k : 256 * k + 256] for k in range(4)], axis=0)
    other_core = lax.ppermute(own_w, "sub", [(i, i ^ 1) for i in range(16)])
    other_y = lax.ppermute(own_w, "sub", [(i, i ^ 2) for i in range(16)])
    other_both = lax.ppermute(other_y, "sub", [(i, i ^ 1) for i in range(16)])

    block = lax.all_gather(frames, "sub", axis=0, tiled=True, axis_index_groups=J_GROUPS)

    order = [2, 3, 4, 5, 6, 7, 0, 1]
    ups = jnp.stack([w_upsample[t] for t in order], axis=1)
    ups = ups.reshape(96, 8, 16, 48).transpose(2, 0, 1, 3).reshape(16 * 96, 384)
    ups = lax.all_to_all(ups, "sub", 0, 0, tiled=True)

    first_norm = norm_rows(block, modulation[0], modulation[1]).astype(bf16)
    projected = mm_t(first_norm, w_att).astype(bf16)
    kv = projected.reshape(256, 4, 256)[:, :, :128].reshape(256, 512)
    back = lax.ppermute(kv, both, [(i, i + 4) for i in range(n_all - 4)])
    is_first = (time_index == 0) & (sub_index < 4)
    partial = attention(is_first.astype(jnp.int32).reshape(1), projected, back, w_att)
    parts = lax.all_to_all(partial, "sub", 0, 0, tiled=True, axis_index_groups=J_GROUPS)
    attn = jnp.sum(parts.reshape(4, own_rows, 1024).astype(f32), axis=0)
    mixed_rows = (frames.astype(f32) + modulation[2] * attn).astype(bf16)
    own_norm = norm_rows(mixed_rows, modulation[3], modulation[4]).astype(bf16)

    second = lax.all_gather(own_norm, "sub", axis=0, tiled=True, axis_index_groups=X_GROUPS)
    partial = mlp(second, (own_w, other_core, other_y, other_both))
    parts = lax.all_to_all(partial, "sub", 0, 0, tiled=True, axis_index_groups=X_GROUPS)
    feed = jnp.sum(parts.reshape(4, own_rows, 1024).astype(f32), axis=0)
    final_rows = (mixed_rows.astype(f32) + modulation[5] * feed).astype(bf16)
    final_norm = norm_rows(final_rows, modulation[6], modulation[7]).astype(bf16)
    velocity = mm(final_norm, w_velocity)
    noisy_own = lax.dynamic_slice_in_dim(noisy_mel, sub_index * own_rows, own_rows, 0)
    mel_own = noisy_own + 0.5 * velocity
    copies = jnp.broadcast_to(mel_own[None], (n_sub,) + mel_own.shape)
    mel_next = lax.all_to_all(copies, "sub", 0, 0).reshape(-1, mel_own.shape[1])

    pre_all = w_voc[:, :96, :].reshape(1536, 768)
    comp = lax.dot_general(pre_all, ups, (((0,), (0,)), ((), ())), preferred_element_type=f32)
    comp = jnp.pad(comp[:700].reshape(7, 100, 384), ((0, 0), (0, MEL_PAD - 100), (0, 0)))
    here, near = comp[:, :, :192], comp[:, :, 192:]
    earlier = lax.broadcasted_iota(jnp.int32, (1, 1, 192), 2) < 96

    def placed(values, start):
        return jnp.pad(values, ((start, OFFSETS - 7 - start), (0, 0), (0, 0)))

    w_here = placed(here, 1)
    w_full = w_here + jnp.where(earlier, placed(near, 0), placed(near, 2))
    w_here = w_here.astype(bf16).reshape(OFFSETS * MEL_PAD, 192)
    w_full = w_full.astype(bf16).reshape(OFFSETS * MEL_PAD, 192)

    mel_low = jnp.pad(mel_next.astype(bf16), ((0, 0), (0, MEL_PAD - 100)))
    count = mel_low.shape[0]
    before = lax.ppermute(mel_low[count - HALO :], "tm", [(i, i + 1) for i in range(n_tm - 1)])
    after = lax.ppermute(mel_low[:HALO], "tm", [(i + 1, i) for i in range(n_tm - 1)])
    mel_ext = jnp.concatenate([before, mel_low, after], axis=0)
    span = count + 2
    cols = jnp.concatenate([mel_ext[3 + k : 3 + k + span] for k in range(OFFSETS)], axis=1)
    up = mm(cols, w_full)
    edge_cols = jnp.concatenate([cols[1:2], cols[count : count + 1]], axis=0)
    edge = mm(edge_cols, w_here)
    row = lax.broadcasted_iota(jnp.int32, (span, 1), 0)
    at_start = (time_index == 0) & (row == 1) & earlier[0]
    at_end = (time_index == n_tm - 1) & (row == count) & jnp.logical_not(earlier[0])
    up = jnp.where(at_start, edge[0:1], jnp.where(at_end, edge[1:2], up)).astype(bf16)
    windows = jnp.stack([up[64 * s : 64 * s + 66] for s in range(16)], axis=0)
    windows = jnp.pad(windows, ((0, 0), (0, ROWS - 66), (0, 0)))
    up_x = lax.all_to_all(windows, "sub", 0, 0, tiled=True)

    here_index = time_index * n_sub + sub_index
    flags = jnp.stack([here_index == 0, here_index == n_all - 1]).astype(jnp.int32)
    out = convolutions(flags, up_x, snake_alpha, w_voc)
    return (mel_next, out.reshape(256, 768))


def solution(mesh):
    in_specs = (
        P(("tm", "sub"), None),
        P(),
        P(None, None, "sub"),
        P("sub", None),
        P(None, "sub"),
        P("sub", None),
        P(),
        P("tm", None),
        P(None, "sub", None),
        P(None, "sub", None),
        P(),
        P(None, "sub", None),
        P(None, "sub", None),
    )
    out_specs = (P("tm", None), P(("tm", "sub"), None))
    return jax.shard_map(body, mesh=mesh, in_specs=in_specs, out_specs=out_specs, check_vma=False)
```

```python
import math

import jax
import jax.numpy as jnp
from jax import lax
from jax.experimental import pallas as pl
from jax.experimental.pallas import tpu as pltpu
from jax.sharding import PartitionSpec as P


HEAD_DIM = 64
BLK = 256
MEL_PAD = 128
OFFSETS = 9

epsilon = 1e-06
bf16 = jnp.bfloat16
f32 = jnp.float32

X_GROUPS = [[4 * x + j for x in range(4)] for j in range(4)]
J_GROUPS = [[4 * x + j for j in range(4)] for x in range(4)]


def norm_rows(rows, offset_row, scale_row):
    rows = rows.astype(f32)
    center = jnp.mean(rows, axis=-1, keepdims=True)
    square = jnp.mean(rows * rows, axis=-1, keepdims=True)
    spread = square - center * center
    return (rows - center) * lax.rsqrt(spread + epsilon) * (1.0 + scale_row) + offset_row


def mm(a, b):
    return jnp.dot(a, b, preferred_element_type=f32)


def mm_t(a, b):
    return lax.dot_general(a, b, (((1,), (1,)), ((), ())), preferred_element_type=f32)


def vmem_specs(n):
    return [pl.BlockSpec(memory_space=pltpu.VMEM)] * n


def whole(kernel, out_shapes, args, scratch=(), cost=None, smem=0, vmem=24):
    single = not isinstance(out_shapes, (tuple, list))
    return pl.pallas_call(
        kernel,
        out_shape=out_shapes,
        in_specs=[pl.BlockSpec(memory_space=pltpu.SMEM)] * smem + vmem_specs(len(args) - smem),
        out_specs=vmem_specs(1)[0] if single else vmem_specs(len(out_shapes)),
        scratch_shapes=list(scratch),
        compiler_params=pltpu.CompilerParams(vmem_limit_bytes=vmem << 20),
        cost_estimate=cost,
    )(*args)


def cost_of(flops, nbytes, trans=0):
    return pl.CostEstimate(flops=flops, bytes_accessed=nbytes, transcendentals=trans)


def attention_weights_kernel(w_ref, o_ref, out_ref):
    for k in range(3):
        out_ref[64 * k : 64 * k + 64, :] = w_ref[k]
    out_ref[192:256, :] = o_ref[...]


def mlp_weights_kernel(up_ref, down_ref, out_ref):
    out_ref[0:1024, :] = up_ref[...]
    for k in range(4):
        out_ref[1024 + 256 * k : 1280 + 256 * k, :] = down_ref[:, 256 * k : 256 * k + 256]


def vocoder_weights_kernel(pre_ref, dil_ref, plain_ref, out_ref):
    out_ref[0:96, :] = jnp.zeros((96, 768), bf16)
    for k in range(7):
        out_ref[0:96, 100 * k : 100 * k + 100] = pre_ref[k]
    for k in range(3):
        out_ref[96 + 48 * k : 144 + 48 * k, :] = dil_ref[k]
        out_ref[240 + 48 * k : 288 + 48 * k, :] = plain_ref[k]


TAP_ORDER = (2, 3, 4, 5, 6, 7, 0, 1)


def upsample_weights_kernel(w_ref, out_ref):
    for s in range(16):
        for t, tap in enumerate(TAP_ORDER):
            out_ref[s, :, 48 * t : 48 * t + 48] = w_ref[tap, :, 48 * s : 48 * s + 48]


def attention_kernel(
    flag_ref, own_ref, back_ref, mod_ref, w0, w1, w2, w3a, w3b, out_ref, heads, w_out
):
    first = flag_ref[0] > 0
    scale = 1.0 / math.sqrt(HEAD_DIM)
    shift, gain = mod_ref[0:1, :], mod_ref[1:2, :]
    own = norm_rows(own_ref[...], shift, gain).astype(bf16)
    back = norm_rows(back_ref[...], shift, gain).astype(bf16)
    for h, (wa, wb, base) in enumerate(((w0, w0, 128), (w1, w1, 128), (w2, w2, 128), (w3a, w3b, 0))):
        qk = mm_t(own, wa[0:128, :]).astype(bf16)
        q, k = qk[:, 0:64], qk[:, 64:128]
        v = mm_t(own, wb[base : base + 64, :]).astype(bf16)
        kb = mm_t(back, wa[64:128, :]).astype(bf16)
        vb = mm_t(back, wb[base : base + 64, :]).astype(bf16)
        s_own = mm_t(q, k) * scale
        s_back = mm_t(q, kb) * scale
        s_back = jnp.where(first, -1e30, s_back)
        top = jnp.maximum(
            jnp.max(s_own, axis=-1, keepdims=True), jnp.max(s_back, axis=-1, keepdims=True)
        )
        e_own = jnp.exp(s_own - top)
        e_back = jnp.exp(s_back - top)
        total = jnp.sum(e_own, axis=-1, keepdims=True) + jnp.sum(e_back, axis=-1, keepdims=True)
        inv = 1.0 / total
        p_own = (e_own * inv).astype(bf16)
        p_back = (e_back * inv).astype(bf16)
        heads[:, 64 * h : 64 * h + 64] = (mm(p_own, v) + mm(p_back, vb)).astype(bf16)
        w_out[64 * h : 64 * h + 64, :] = wb[base + 64 : base + 128, :]
    out_ref[...] = mm(heads[...], w_out[...]).astype(bf16)


def after_attention_kernel(parts_ref, frames_ref, mod_ref, mixed_ref, norm_ref):
    attn = parts_ref[0].astype(f32)
    for k in range(1, 4):
        attn += parts_ref[k].astype(f32)
    mixed = (frames_ref[...].astype(f32) + mod_ref[2:3, :] * attn).astype(bf16)
    mixed_ref[...] = mixed
    norm_ref[...] = norm_rows(mixed, mod_ref[3:4, :], mod_ref[4:5, :]).astype(bf16)


def mlp_kernel(h_ref, w0, w1, w2, w3, out_ref, acc):
    h = h_ref[...]
    for i, w in enumerate((w0, w1, w2, w3)):
        up = mm(h, w[0:1024, :])
        hid = jax.nn.gelu(up, approximate=True).astype(bf16)
        for k in range(4):
            part = mm(hid, w[1024 + 256 * k : 1280 + 256 * k, :])
            cols = slice(256 * k, 256 * k + 256)
            if i == 0:
                acc[:, cols] = part
            elif i < 3:
                acc[:, cols] += part
            else:
                out_ref[:, cols] = (acc[:, cols] + part).astype(bf16)


def after_mlp_kernel(parts_ref, mixed_ref, mod_ref, wv_ref, noisy_ref, out_ref):
    feed = parts_ref[0].astype(f32)
    for k in range(1, 4):
        feed += parts_ref[k].astype(f32)
    final = (mixed_ref[...].astype(f32) + mod_ref[5:6, :] * feed).astype(bf16)
    normed = norm_rows(final, mod_ref[6:7, :], mod_ref[7:8, :]).astype(bf16)
    mel = noisy_ref[...] + 0.5 * mm(normed, wv_ref[...])
    for s in range(16):
        out_ref[s] = mel


def placed_kernel(comp_ref, full_ref, here_ref):
    earlier = lax.broadcasted_iota(jnp.int32, (100, 192), 1) < 96
    full_ref[...] = jnp.zeros(full_ref.shape, bf16)
    here_ref[...] = jnp.zeros(here_ref.shape, bf16)
    here = [comp_ref[100 * j : 100 * j + 100, 0:192] for j in range(7)]
    near = [comp_ref[100 * j : 100 * j + 100, 192:384] for j in range(7)]
    for d in range(OFFSETS):
        value = jnp.zeros((100, 192), f32)
        if 0 <= d - 1 < 7:
            value = here[d - 1]
            here_ref[MEL_PAD * d : MEL_PAD * d + 100, :] = value.astype(bf16)
        if d < 7:
            value = value + jnp.where(earlier, near[d], 0.0)
        if 0 <= d - 2 < 7:
            value = value + jnp.where(earlier, 0.0, near[d - 2])
        full_ref[MEL_PAD * d : MEL_PAD * d + 100, :] = value.astype(bf16)


EXT = 1056


def upsample_kernel(flag_ref, mel_ref, before_ref, after_ref, full_ref, here_ref, out_ref, ext, up):
    ext[...] = jnp.zeros((EXT, MEL_PAD), f32)
    ext[0:8, 0:100] = before_ref[...]
    for s in range(16):
        ext[8 + 64 * s : 72 + 64 * s, 0:100] = mel_ref[s]
    ext[1032:1040, 0:100] = after_ref[...]
    cols = [ext[3 + k : 3 + k + 1032, :].astype(bf16) for k in range(OFFSETS)]
    up[...] = mm(jnp.concatenate(cols, axis=1), full_ref[...])
    earlier = lax.broadcasted_iota(jnp.int32, (8, 192), 1) < 96
    row = lax.broadcasted_iota(jnp.int32, (8, 192), 0)
    for which, base, r in ((0, 0, 1), (1, 1024, 0)):
        edge_cols = [ext[base + 3 + k : base + 11 + k, :].astype(bf16) for k in range(OFFSETS)]
        edge = mm(jnp.concatenate(edge_cols, axis=1), here_ref[...])
        lanes = earlier if which == 0 else jnp.logical_not(earlier)
        use = (flag_ref[which] > 0) & (row == r) & lanes
        up[base : base + 8, :] = jnp.where(use, edge, up[base : base + 8, :])
    for s in range(16):
        out_ref[s] = up[64 * s : 64 * s + ROWS, :].astype(bf16)


PI_PARTS = (3.140625, 0.000965118408203125, 2.5331974029541016e-06, 1.984187258941006e-09)


def sin_squared(x):
    k = jnp.round(x * (1.0 / math.pi))
    r = x
    for part in PI_PARTS:
        r = r - k * part
    z = r * r
    poly = -2.3889859e-08 * z + 2.7525562e-06
    poly = poly * z - 1.9840874e-04
    poly = poly * z + 8.3333310e-03
    poly = poly * z - 1.6666667e-01
    sine = r + r * (z * poly)
    return sine * sine


def snake_act(values, alpha_row, inverse_row):
    return values + sin_squared(alpha_row * values) * inverse_row


def shifted(plane, by):
    return pltpu.roll(plane, by % plane.shape[0], 0)


ROWS = 72


def conv_kernel(flag_ref, up_ref, alpha_ref, w_ref, out_ref, planes):
    first = flag_ref[0] > 0
    last = flag_ref[1] > 0
    row = lax.broadcasted_iota(jnp.int32, (ROWS, 768), 0)
    outside = (first & (row == 0)) | (last & (row == 65))
    for s in range(16):
        for p in range(4):
            planes[p, :, 48 * s : 48 * s + 48] = up_ref[s, :, 48 * p : 48 * p + 48]
    a1 = alpha_ref[0:1, :]
    a2 = alpha_ref[1:2, :]
    i1 = 1.0 / a1
    i2 = 1.0 / a2

    def weight(base, tap):
        return jnp.concatenate(
            [w_ref[s, base + 48 * tap : base + 48 * tap + 48, :] for s in range(16)], axis=0
        )

    ups = []
    acts = []
    for p in range(4):
        u = jnp.where(outside, 0.0, planes[p].astype(f32))
        ups.append(u)
        acts.append(snake_act(u, a1, i1).astype(bf16))
    act = jnp.concatenate(acts, axis=0)
    y = [mm(act, weight(96, tap)) for tap in range(3)]
    y = [[v[ROWS * p : ROWS * p + ROWS] for p in range(4)] for v in y]
    acts = []
    for p in range(4):
        before = y[0][0] if p == 3 else shifted(y[0][p + 1], 1)
        after = y[2][3] if p == 0 else shifted(y[2][p - 1], -1)
        inner = before + y[1][p] + after
        acts.append(jnp.where(outside, 0.0, snake_act(inner, a2, i2)).astype(bf16))
    act = jnp.concatenate(acts, axis=0)
    y = [mm(act, weight(240, tap)) for tap in range(3)]
    y = [[v[ROWS * p : ROWS * p + ROWS] for p in range(4)] for v in y]
    for p in range(4):
        before = y[0][p - 1] if p >= 1 else shifted(y[0][3], 1)
        after = y[2][p + 1] if p <= 2 else shifted(y[2][0], -1)
        total = ups[p] + (before + y[1][p] + after)
        out_ref[:, 768 * p : 768 * p + 768] = shifted(total, -1)[0:64].astype(bf16)


def gather(value, groups):
    return lax.all_gather(value, "sub", axis=0, tiled=True, axis_index_groups=groups)


def exchange(value, groups=None):
    return lax.all_to_all(value, "sub", 0, 0, tiled=True, axis_index_groups=groups)


def device(y_hi, z, x, y_lo, core):
    return (y_hi * 8 + z) * 16 + x * 4 + y_lo * 2 + core


OTHER_Y = [
    (device(h, z, x, y, c), device(1 - h, z, x, 1 - y, c))
    for h in range(2)
    for z in range(8)
    for x in range(4)
    for y in range(2)
    for c in range(2)
]


def program(
    frames,
    modulation,
    w_project,
    w_heads_out,
    w_up,
    w_down,
    w_velocity,
    noisy_mel,
    w_prelude,
    w_upsample,
    snake_alpha,
    w_dilated,
    w_plain,
):
    own_rows = frames.shape[0]
    sub_index = lax.axis_index("sub")
    time_index = lax.axis_index("tm")
    n_sub = lax.axis_size("sub")
    n_tm = lax.axis_size("tm")
    n_all = n_sub * n_tm
    both = ("tm", "sub")
    shape = jax.ShapeDtypeStruct
    here_index = time_index * n_sub + sub_index

    to_right = [(i, (i + 4) % 16) for i in range(16)]
    to_left = [(i, (i - 4) % 16) for i in range(16)]
    w_own = whole(
        attention_weights_kernel,
        shape((256, 1024), bf16),
        (jnp.swapaxes(w_project, 1, 2), w_heads_out),
        cost=cost_of(0, 1 << 20),
    )
    back_frames = lax.ppermute(frames, both, [(i, i + 4) for i in range(n_all - 4)])
    from_left = lax.ppermute(w_own, "sub", to_right)
    from_right = lax.ppermute(w_own, "sub", to_left)

    w_voc = whole(
        vocoder_weights_kernel,
        shape((384, 768), bf16),
        lax.optimization_barrier((w_prelude, w_dilated, w_plain, w_own))[:3],
        cost=cost_of(0, 2 << 20),
    )
    w_voc = lax.all_gather(w_voc, "sub", axis=0, tiled=False)

    block = gather(frames, J_GROUPS)
    far_a = lax.ppermute(from_left[:128], "sub", to_right)
    far_b = lax.ppermute(from_right[128:], "sub", to_left)
    back = gather(back_frames, J_GROUPS)

    own_mlp = whole(
        mlp_weights_kernel, shape((2048, 256), bf16), (w_up, w_down), cost=cost_of(0, 2 << 20)
    )
    other_core = lax.ppermute(own_mlp, "sub", [(i, i ^ 1) for i in range(16)])
    other_y = lax.ppermute(own_mlp, both, OTHER_Y)
    other_both = lax.ppermute(other_y, "sub", [(i, i ^ 1) for i in range(16)])

    ups = whole(
        upsample_weights_kernel, shape((16, 96, 384), bf16), (w_upsample,), cost=cost_of(0, 3 << 20)
    )

    is_first = (time_index == 0) & (sub_index < 4)
    partial = whole(
        attention_kernel,
        shape((BLK, 1024), bf16),
        (
            is_first.astype(jnp.int32).reshape(1),
            block,
            back,
            modulation,
            w_own,
            from_left,
            from_right,
            far_a,
            far_b,
        ),
        scratch=[pltpu.VMEM((BLK, 256), bf16), pltpu.VMEM((256, 1024), bf16)],
        cost=cost_of(10**9, 4 << 20, 1 << 19),
        smem=1,
    )
    ups = exchange(ups)
    partial, ups = lax.optimization_barrier((partial, ups))
    parts = exchange(partial, J_GROUPS)
    mixed_rows, own_norm = whole(
        after_attention_kernel,
        (shape((own_rows, 1024), bf16), shape((own_rows, 1024), bf16)),
        (parts.reshape(4, own_rows, 1024), frames, modulation),
        cost=cost_of(10**6, 1 << 20),
    )

    second = gather(own_norm, X_GROUPS)
    partial = whole(
        mlp_kernel,
        shape((256, 1024), bf16),
        (second, own_mlp, other_core, other_y, other_both),
        scratch=[pltpu.VMEM((256, 1024), f32)],
        cost=cost_of(11 * 10**8, 5 << 20, 1 << 18),
    )
    parts = exchange(partial, X_GROUPS)
    noisy_own = lax.dynamic_slice_in_dim(noisy_mel, sub_index * own_rows, own_rows, 0)
    copies = whole(
        after_mlp_kernel,
        shape((16, own_rows, 100), f32),
        (parts.reshape(4, own_rows, 1024), mixed_rows, modulation, w_velocity, noisy_own),
        cost=cost_of(10**7, 1 << 20),
    )
    mel_all = exchange(copies)
    mel_next = mel_all.reshape(-1, 100)

    pre_all = w_voc[:, :96, :].reshape(1536, 768)
    comp = lax.dot_general(
        pre_all, ups.reshape(1536, 384), (((0,), (0,)), ((), ())), preferred_element_type=f32
    )
    w_full, w_here = whole(
        placed_kernel,
        (shape((OFFSETS * MEL_PAD, 192), bf16), shape((OFFSETS * MEL_PAD, 192), bf16)),
        (comp,),
        cost=cost_of(10**6, 2 << 20),
    )

    before = lax.ppermute(mel_all[15, 56:], "tm", [(i, i + 1) for i in range(n_tm - 1)])
    after = lax.ppermute(mel_all[0, :8], "tm", [(i + 1, i) for i in range(n_tm - 1)])
    windows = whole(
        upsample_kernel,
        shape((16, ROWS, 192), bf16),
        (
            jnp.stack([time_index == 0, time_index == n_tm - 1]).astype(jnp.int32),
            mel_all,
            before,
            after,
            w_full,
            w_here,
        ),
        scratch=[pltpu.VMEM((EXT, MEL_PAD), f32), pltpu.VMEM((1032, 192), f32)],
        cost=cost_of(5 * 10**8, 2 << 20),
        smem=1,
    )
    up_x = exchange(windows)

    flags = jnp.stack([here_index == 0, here_index == n_all - 1]).astype(jnp.int32)
    out = whole(
        conv_kernel,
        shape((64, 3072), bf16),
        (flags, up_x, snake_alpha, w_voc),
        scratch=[pltpu.VMEM((4, ROWS, 768), bf16)],
        cost=cost_of(2 * 10**9, 8 << 20, 1 << 18),
        smem=1,
        vmem=32,
    )
    return (mel_next, out.reshape(256, 768))


def solution(mesh):
    in_specs = (
        P(("tm", "sub"), None),
        P(),
        P(None, None, "sub"),
        P("sub", None),
        P(None, "sub"),
        P("sub", None),
        P(),
        P("tm", None),
        P(None, "sub", None),
        P(None, "sub", None),
        P(),
        P(None, "sub", None),
        P(None, "sub", None),
    )
    out_specs = (P("tm", None), P(("tm", "sub"), None))
    return jax.shard_map(program, mesh=mesh, in_specs=in_specs, out_specs=out_specs, check_vma=False)
```

```python
import math

import jax
import jax.numpy as jnp
from jax import lax
from jax.experimental import pallas as pl
from jax.experimental.pallas import tpu as pltpu
from jax.sharding import PartitionSpec as P


HEAD_DIM = 64
BLK = 256
MEL_PAD = 128
OFFSETS = 9

epsilon = 1e-06
bf16 = jnp.bfloat16
f32 = jnp.float32

X_GROUPS = [[4 * x + j for x in range(4)] for j in range(4)]
J_GROUPS = [[4 * x + j for j in range(4)] for x in range(4)]


def norm_rows(rows, offset_row, scale_row):
    rows = rows.astype(f32)
    center = jnp.mean(rows, axis=-1, keepdims=True)
    square = jnp.mean(rows * rows, axis=-1, keepdims=True)
    spread = square - center * center
    return (rows - center) * lax.rsqrt(spread + epsilon) * (1.0 + scale_row) + offset_row


def mm(a, b):
    return jnp.dot(a, b, preferred_element_type=f32)


def mm_t(a, b):
    return lax.dot_general(a, b, (((1,), (1,)), ((), ())), preferred_element_type=f32)


def vmem_specs(n):
    return [pl.BlockSpec(memory_space=pltpu.VMEM)] * n


def whole(kernel, out_shapes, args, scratch=(), cost=None, smem=0, vmem=24):
    single = not isinstance(out_shapes, (tuple, list))
    return pl.pallas_call(
        kernel,
        out_shape=out_shapes,
        in_specs=[pl.BlockSpec(memory_space=pltpu.SMEM)] * smem + vmem_specs(len(args) - smem),
        out_specs=vmem_specs(1)[0] if single else vmem_specs(len(out_shapes)),
        scratch_shapes=list(scratch),
        compiler_params=pltpu.CompilerParams(vmem_limit_bytes=vmem << 20),
        cost_estimate=cost,
    )(*args)


def cost_of(flops, nbytes, trans=0):
    return pl.CostEstimate(flops=flops, bytes_accessed=nbytes, transcendentals=trans)


def attention_weights_kernel(w_ref, o_ref, a_ref, b_ref):
    a_ref[0:64, :] = w_ref[0]
    a_ref[64:128, :] = w_ref[1]
    b_ref[0:64, :] = w_ref[2]
    b_ref[64:128, :] = o_ref[...]


def mlp_weights_kernel(up_ref, down_ref, out_ref):
    out_ref[0:1024, :] = up_ref[...]
    for k in range(4):
        out_ref[1024 + 256 * k : 1280 + 256 * k, :] = down_ref[:, 256 * k : 256 * k + 256]


def vocoder_weights_kernel(pre_ref, dil_ref, plain_ref, out_ref):
    out_ref[0:96, :] = jnp.zeros((96, 768), bf16)
    for k in range(7):
        out_ref[0:96, 100 * k : 100 * k + 100] = pre_ref[k]
    for k in range(3):
        out_ref[96 + 48 * k : 144 + 48 * k, :] = dil_ref[k]
        out_ref[240 + 48 * k : 288 + 48 * k, :] = plain_ref[k]


TAP_ORDER = (2, 3, 4, 5, 6, 7, 0, 1)


def upsample_weights_kernel(w_ref, out_ref):
    for s in range(16):
        for t, tap in enumerate(TAP_ORDER):
            out_ref[s, :, 48 * t : 48 * t + 48] = w_ref[tap, :, 48 * s : 48 * s + 48]


def attention_kernel(
    flag_ref, own_ref, back_ref, mod_ref, a0, b0, a1, b1, a2, b2, a3, b3, out_ref, heads, w_out
):
    first = flag_ref[0] > 0
    scale = 1.0 / math.sqrt(HEAD_DIM)
    shift, gain = mod_ref[0:1, :], mod_ref[1:2, :]
    own = norm_rows(own_ref[...], shift, gain).astype(bf16)
    back = norm_rows(back_ref[...], shift, gain).astype(bf16)
    for h, (wa, wb) in enumerate(((a0, b0), (a1, b1), (a2, b2), (a3, b3))):
        qk = mm_t(own, wa[0:128, :]).astype(bf16)
        q, k = qk[:, 0:64], qk[:, 64:128]
        v = mm_t(own, wb[0:64, :]).astype(bf16)
        kb = mm_t(back, wa[64:128, :]).astype(bf16)
        vb = mm_t(back, wb[0:64, :]).astype(bf16)
        s_own = mm_t(q, k) * scale
        s_back = mm_t(q, kb) * scale
        s_back = jnp.where(first, -1e30, s_back)
        top = jnp.maximum(
            jnp.max(s_own, axis=-1, keepdims=True), jnp.max(s_back, axis=-1, keepdims=True)
        )
        e_own = jnp.exp(s_own - top)
        e_back = jnp.exp(s_back - top)
        total = jnp.sum(e_own, axis=-1, keepdims=True) + jnp.sum(e_back, axis=-1, keepdims=True)
        inv = 1.0 / total
        p_own = (e_own * inv).astype(bf16)
        p_back = (e_back * inv).astype(bf16)
        heads[:, 64 * h : 64 * h + 64] = (mm(p_own, v) + mm(p_back, vb)).astype(bf16)
        w_out[64 * h : 64 * h + 64, :] = wb[64:128, :]
    out_ref[...] = mm(heads[...], w_out[...]).astype(bf16)


def after_attention_kernel(parts_ref, frames_ref, mod_ref, mixed_ref, norm_ref):
    attn = parts_ref[0].astype(f32)
    for k in range(1, 4):
        attn += parts_ref[k].astype(f32)
    mixed = (frames_ref[...].astype(f32) + mod_ref[2:3, :] * attn).astype(bf16)
    mixed_ref[...] = mixed
    norm_ref[...] = norm_rows(mixed, mod_ref[3:4, :], mod_ref[4:5, :]).astype(bf16)


def mlp_kernel(h_ref, w0, w1, w2, w3, out_ref, acc):
    h = h_ref[...]
    for i, w in enumerate((w0, w1, w2, w3)):
        up = mm(h, w[0:1024, :])
        hid = jax.nn.gelu(up, approximate=True).astype(bf16)
        for k in range(4):
            part = mm(hid, w[1024 + 256 * k : 1280 + 256 * k, :])
            cols = slice(256 * k, 256 * k + 256)
            if i == 0:
                acc[:, cols] = part
            elif i < 3:
                acc[:, cols] += part
            else:
                out_ref[:, cols] = (acc[:, cols] + part).astype(bf16)


def after_mlp_kernel(parts_ref, mixed_ref, mod_ref, wv_ref, noisy_ref, out_ref):
    feed = parts_ref[0].astype(f32)
    for k in range(1, 4):
        feed += parts_ref[k].astype(f32)
    final = (mixed_ref[...].astype(f32) + mod_ref[5:6, :] * feed).astype(bf16)
    normed = norm_rows(final, mod_ref[6:7, :], mod_ref[7:8, :]).astype(bf16)
    mel = noisy_ref[...] + 0.5 * mm(normed, wv_ref[...])
    for s in range(16):
        out_ref[s] = mel


def placed_kernel(comp_ref, full_ref, here_ref):
    earlier = lax.broadcasted_iota(jnp.int32, (100, 192), 1) < 96
    full_ref[...] = jnp.zeros(full_ref.shape, bf16)
    here_ref[...] = jnp.zeros(here_ref.shape, bf16)
    here = [comp_ref[100 * j : 100 * j + 100, 0:192] for j in range(7)]
    near = [comp_ref[100 * j : 100 * j + 100, 192:384] for j in range(7)]
    for d in range(OFFSETS):
        value = jnp.zeros((100, 192), f32)
        if 0 <= d - 1 < 7:
            value = here[d - 1]
            here_ref[MEL_PAD * d : MEL_PAD * d + 100, :] = value.astype(bf16)
        if d < 7:
            value = value + jnp.where(earlier, near[d], 0.0)
        if 0 <= d - 2 < 7:
            value = value + jnp.where(earlier, 0.0, near[d - 2])
        full_ref[MEL_PAD * d : MEL_PAD * d + 100, :] = value.astype(bf16)


EXT = 1056


def upsample_kernel(flag_ref, mel_ref, before_ref, after_ref, full_ref, here_ref, out_ref, ext, up):
    ext[...] = jnp.zeros((EXT, MEL_PAD), f32)
    ext[0:8, 0:100] = before_ref[...]
    for s in range(16):
        ext[8 + 64 * s : 72 + 64 * s, 0:100] = mel_ref[s]
    ext[1032:1040, 0:100] = after_ref[...]
    cols = [ext[3 + k : 3 + k + 1032, :].astype(bf16) for k in range(OFFSETS)]
    up[...] = mm(jnp.concatenate(cols, axis=1), full_ref[...])
    earlier = lax.broadcasted_iota(jnp.int32, (8, 192), 1) < 96
    row = lax.broadcasted_iota(jnp.int32, (8, 192), 0)
    for which, base, r in ((0, 0, 1), (1, 1024, 0)):
        edge_cols = [ext[base + 3 + k : base + 11 + k, :].astype(bf16) for k in range(OFFSETS)]
        edge = mm(jnp.concatenate(edge_cols, axis=1), here_ref[...])
        lanes = earlier if which == 0 else jnp.logical_not(earlier)
        use = (flag_ref[which] > 0) & (row == r) & lanes
        up[base : base + 8, :] = jnp.where(use, edge, up[base : base + 8, :])
    for s in range(16):
        out_ref[s] = up[64 * s : 64 * s + ROWS, :].astype(bf16)


PI_PARTS = (3.140625, 0.000965118408203125, 2.5331974029541016e-06, 1.984187258941006e-09)


def sin_squared(x):
    k = jnp.round(x * (1.0 / math.pi))
    r = x
    for part in PI_PARTS:
        r = r - k * part
    z = r * r
    poly = -2.3889859e-08 * z + 2.7525562e-06
    poly = poly * z - 1.9840874e-04
    poly = poly * z + 8.3333310e-03
    poly = poly * z - 1.6666667e-01
    sine = r + r * (z * poly)
    return sine * sine


def snake_act(values, alpha_row, inverse_row):
    return values + sin_squared(alpha_row * values) * inverse_row


def shifted(plane, by):
    return pltpu.roll(plane, by % plane.shape[0], 0)


ROWS = 72


def conv_kernel(flag_ref, up_ref, alpha_ref, w_hbm, out_ref, planes, w_ref, sem):
    copies = [
        pltpu.make_async_copy(
            w_hbm.at[:, pl.ds(96 + 144 * k, 144), :],
            w_ref.at[:, pl.ds(144 * k, 144), :],
            sem.at[k],
        )
        for k in range(2)
    ]
    for c in copies:
        c.start()
    first = flag_ref[0] > 0
    last = flag_ref[1] > 0
    row = lax.broadcasted_iota(jnp.int32, (ROWS, 768), 0)
    outside = (first & (row == 0)) | (last & (row == 65))
    for s in range(16):
        for p in range(4):
            planes[p, :, 48 * s : 48 * s + 48] = up_ref[s, :, 48 * p : 48 * p + 48]
    a1 = alpha_ref[0:1, :]
    a2 = alpha_ref[1:2, :]
    i1 = 1.0 / a1
    i2 = 1.0 / a2

    def weight(base, tap):
        return jnp.concatenate(
            [w_ref[s, base + 48 * tap : base + 48 * tap + 48, :] for s in range(16)], axis=0
        )

    ups = []
    acts = []
    for p in range(4):
        u = jnp.where(outside, 0.0, planes[p].astype(f32))
        ups.append(u)
        acts.append(snake_act(u, a1, i1).astype(bf16))
    act = jnp.concatenate(acts, axis=0)
    copies[0].wait()
    y = [mm(act, weight(0, tap)) for tap in range(3)]
    y = [[v[ROWS * p : ROWS * p + ROWS] for p in range(4)] for v in y]
    acts = []
    for p in range(4):
        before = y[0][0] if p == 3 else shifted(y[0][p + 1], 1)
        after = y[2][3] if p == 0 else shifted(y[2][p - 1], -1)
        inner = before + y[1][p] + after
        acts.append(jnp.where(outside, 0.0, snake_act(inner, a2, i2)).astype(bf16))
    act = jnp.concatenate(acts, axis=0)
    copies[1].wait()
    y = [mm(act, weight(144, tap)) for tap in range(3)]
    y = [[v[ROWS * p : ROWS * p + ROWS] for p in range(4)] for v in y]
    for p in range(4):
        before = y[0][p - 1] if p >= 1 else shifted(y[0][3], 1)
        after = y[2][p + 1] if p <= 2 else shifted(y[2][0], -1)
        total = ups[p] + (before + y[1][p] + after)
        out_ref[:, 768 * p : 768 * p + 768] = shifted(total, -1)[0:64].astype(bf16)


def gather(value, groups):
    return lax.all_gather(value, "sub", axis=0, tiled=True, axis_index_groups=groups)


def exchange(value, groups=None, axis="sub"):
    return lax.all_to_all(value, axis, 0, 0, tiled=True, axis_index_groups=groups)


def device(y_hi, z, x, y_lo, core):
    return (y_hi * 8 + z) * 16 + x * 4 + y_lo * 2 + core


OTHER_Y = [
    (device(h, z, x, y, c), device(1 - h, z, x, 1 - y, c))
    for h in range(2)
    for z in range(8)
    for x in range(4)
    for y in range(2)
    for c in range(2)
]
OTHER_GROUPS = [
    [device(y ^ side, z, x, y, c) for x in range(4) for y in range(2) for c in range(2)]
    for side in range(2)
    for z in range(8)
]


def program(
    frames,
    modulation,
    w_project,
    w_heads_out,
    w_up,
    w_down,
    w_velocity,
    noisy_mel,
    w_prelude,
    w_upsample,
    snake_alpha,
    w_dilated,
    w_plain,
):
    own_rows = frames.shape[0]
    sub_index = lax.axis_index("sub")
    time_index = lax.axis_index("tm")
    n_sub = lax.axis_size("sub")
    n_tm = lax.axis_size("tm")
    n_all = n_sub * n_tm
    both = ("tm", "sub")
    shape = jax.ShapeDtypeStruct
    here_index = time_index * n_sub + sub_index

    to_right = [(i, (i + 4) % 16) for i in range(16)]
    to_left = [(i, (i - 4) % 16) for i in range(16)]
    own_a, own_b = whole(
        attention_weights_kernel,
        (shape((128, 1024), bf16), shape((128, 1024), bf16)),
        (jnp.swapaxes(w_project, 1, 2), w_heads_out),
        cost=cost_of(0, 1 << 20),
    )
    back_frames = lax.ppermute(frames, both, [(i, i + 4) for i in range(n_all - 4)])
    left_a = lax.ppermute(own_a, "sub", to_right)
    right_b = lax.ppermute(own_b, "sub", to_left)
    left_b = lax.ppermute(own_b, "sub", to_right)
    right_a = lax.ppermute(own_a, "sub", to_left)
    far_a = lax.ppermute(left_a, "sub", to_right)
    far_b = lax.ppermute(right_b, "sub", to_left)

    w_voc = whole(
        vocoder_weights_kernel,
        shape((384, 768), bf16),
        lax.optimization_barrier((w_prelude, w_dilated, w_plain, own_a))[:3],
        cost=cost_of(0, 2 << 20),
    )
    w_voc = lax.all_gather(w_voc, "sub", axis=0, tiled=False)

    block = gather(frames, J_GROUPS)
    back = gather(back_frames, J_GROUPS)

    own_mlp = whole(
        mlp_weights_kernel, shape((2048, 256), bf16), (w_up, w_down), cost=cost_of(0, 2 << 20)
    )
    other_core = lax.ppermute(own_mlp, "sub", [(i, i ^ 1) for i in range(16)])
    other_y = lax.ppermute(own_mlp, both, OTHER_Y)
    other_both = lax.ppermute(other_y, "sub", [(i, i ^ 1) for i in range(16)])

    ups = whole(
        upsample_weights_kernel, shape((16, 96, 384), bf16), (w_upsample,), cost=cost_of(0, 3 << 20)
    )

    is_first = (time_index == 0) & (sub_index < 4)
    partial = whole(
        attention_kernel,
        shape((BLK, 1024), bf16),
        (
            is_first.astype(jnp.int32).reshape(1),
            block,
            back,
            modulation,
            own_a,
            own_b,
            left_a,
            left_b,
            right_a,
            right_b,
            far_a,
            far_b,
        ),
        scratch=[pltpu.VMEM((BLK, 256), bf16), pltpu.VMEM((256, 1024), bf16)],
        cost=cost_of(10**9, 4 << 20, 1 << 19),
        smem=1,
    )
    ups = exchange(ups, OTHER_GROUPS, both)
    partial, ups = lax.optimization_barrier((partial, ups))
    parts = exchange(partial, J_GROUPS)
    mixed_rows, own_norm = whole(
        after_attention_kernel,
        (shape((own_rows, 1024), bf16), shape((own_rows, 1024), bf16)),
        (parts.reshape(4, own_rows, 1024), frames, modulation),
        cost=cost_of(10**6, 1 << 20),
    )

    second = gather(own_norm, X_GROUPS)
    partial = whole(
        mlp_kernel,
        shape((256, 1024), bf16),
        (second, own_mlp, other_core, other_y, other_both),
        scratch=[pltpu.VMEM((256, 1024), f32)],
        cost=cost_of(11 * 10**8, 5 << 20, 1 << 18),
    )
    parts = exchange(partial, X_GROUPS)
    noisy_own = lax.dynamic_slice_in_dim(noisy_mel, sub_index * own_rows, own_rows, 0)
    copies = whole(
        after_mlp_kernel,
        shape((16, own_rows, 100), f32),
        (parts.reshape(4, own_rows, 1024), mixed_rows, modulation, w_velocity, noisy_own),
        cost=cost_of(10**7, 1 << 20),
    )
    mel_all = exchange(copies)
    mel_next = mel_all.reshape(-1, 100)

    pre_all = w_voc[:, :96, :].reshape(1536, 768)
    comp = lax.dot_general(
        pre_all, ups.reshape(1536, 384), (((0,), (0,)), ((), ())), preferred_element_type=f32
    )
    w_full, w_here = whole(
        placed_kernel,
        (shape((OFFSETS * MEL_PAD, 192), bf16), shape((OFFSETS * MEL_PAD, 192), bf16)),
        (comp,),
        cost=cost_of(10**6, 2 << 20),
    )

    before = lax.ppermute(mel_all[15, 56:], "tm", [(i, i + 1) for i in range(n_tm - 1)])
    after = lax.ppermute(mel_all[0, :8], "tm", [(i + 1, i) for i in range(n_tm - 1)])
    windows = whole(
        upsample_kernel,
        shape((16, ROWS, 192), bf16),
        (
            jnp.stack([time_index == 0, time_index == n_tm - 1]).astype(jnp.int32),
            mel_all,
            before,
            after,
            w_full,
            w_here,
        ),
        scratch=[pltpu.VMEM((EXT, MEL_PAD), f32), pltpu.VMEM((1032, 192), f32)],
        cost=cost_of(5 * 10**8, 2 << 20),
        smem=1,
    )
    up_x = exchange(windows)

    flags = jnp.stack([here_index == 0, here_index == n_all - 1]).astype(jnp.int32)
    out = pl.pallas_call(
        conv_kernel,
        out_shape=shape((64, 3072), bf16),
        in_specs=[pl.BlockSpec(memory_space=pltpu.SMEM)]
        + vmem_specs(2)
        + [pl.BlockSpec(memory_space=pltpu.MemorySpace.HBM)],
        out_specs=pl.BlockSpec(memory_space=pltpu.VMEM),
        scratch_shapes=[
            pltpu.VMEM((4, ROWS, 768), bf16),
            pltpu.VMEM((16, 288, 768), bf16),
            pltpu.SemaphoreType.DMA((2,)),
        ],
        compiler_params=pltpu.CompilerParams(vmem_limit_bytes=54 << 20),
        cost_estimate=cost_of(2 * 10**9, 8 << 20, 1 << 18),
        name="convolutions",
    )(flags, up_x, snake_alpha, w_voc)
    return (mel_next, out.reshape(256, 768))


def solution(mesh):
    in_specs = (
        P(("tm", "sub"), None),
        P(),
        P(None, None, "sub"),
        P("sub", None),
        P(None, "sub"),
        P("sub", None),
        P(),
        P("tm", None),
        P(None, "sub", None),
        P(None, "sub", None),
        P(),
        P(None, "sub", None),
        P(None, "sub", None),
    )
    out_specs = (P("tm", None), P(("tm", "sub"), None))
    return jax.shard_map(program, mesh=mesh, in_specs=in_specs, out_specs=out_specs, check_vma=False)
```

```python
import math

import jax
import jax.numpy as jnp
from jax import lax
from jax.experimental import pallas as pl
from jax.experimental.pallas import tpu as pltpu
from jax.sharding import PartitionSpec as P


HEAD_DIM = 64
BLK = 256
MEL_PAD = 128
OFFSETS = 9

epsilon = 1e-06
bf16 = jnp.bfloat16
f32 = jnp.float32

J_GROUPS = [[4 * x + j for j in range(4)] for x in range(4)]


def norm_rows(rows, offset_row, scale_row):
    rows = rows.astype(f32)
    center = jnp.mean(rows, axis=-1, keepdims=True)
    square = jnp.mean(rows * rows, axis=-1, keepdims=True)
    spread = square - center * center
    return (rows - center) * lax.rsqrt(spread + epsilon) * (1.0 + scale_row) + offset_row


def mm(a, b):
    return jnp.dot(a, b, preferred_element_type=f32)


def mm_t(a, b):
    return lax.dot_general(a, b, (((1,), (1,)), ((), ())), preferred_element_type=f32)


def vmem_specs(n):
    return [pl.BlockSpec(memory_space=pltpu.VMEM)] * n


def whole(kernel, out_shapes, args, scratch=(), cost=None, smem=0, vmem=24):
    single = not isinstance(out_shapes, (tuple, list))
    return pl.pallas_call(
        kernel,
        out_shape=out_shapes,
        in_specs=[pl.BlockSpec(memory_space=pltpu.SMEM)] * smem + vmem_specs(len(args) - smem),
        out_specs=vmem_specs(1)[0] if single else vmem_specs(len(out_shapes)),
        scratch_shapes=list(scratch),
        compiler_params=pltpu.CompilerParams(vmem_limit_bytes=vmem << 20),
        cost_estimate=cost,
    )(*args)


def cost_of(flops, nbytes, trans=0):
    return pl.CostEstimate(flops=flops, bytes_accessed=nbytes, transcendentals=trans)


def first_weights_kernel(w_ref, o_ref, pre_ref, dil_ref, plain_ref, a_ref, b_ref, voc_ref):
    a_ref[0:64, :] = w_ref[0]
    a_ref[64:128, :] = w_ref[1]
    b_ref[0:64, :] = w_ref[2]
    b_ref[64:128, :] = o_ref[...]
    voc_ref[0:96, :] = jnp.zeros((96, 768), bf16)
    for k in range(7):
        voc_ref[0:96, 100 * k : 100 * k + 100] = pre_ref[k]
    for k in range(3):
        voc_ref[96 + 48 * k : 144 + 48 * k, :] = dil_ref[k]
        voc_ref[240 + 48 * k : 288 + 48 * k, :] = plain_ref[k]


def mlp_weights_kernel(up_ref, down_ref, out_ref):
    out_ref[0:1024, :] = up_ref[...]
    for k in range(4):
        out_ref[1024 + 256 * k : 1280 + 256 * k, :] = down_ref[:, 256 * k : 256 * k + 256]


TAP_ORDER = (2, 3, 4, 5, 6, 7, 0, 1)


def upsample_weights_kernel(w_ref, out_ref):
    for s in range(16):
        for t, tap in enumerate(TAP_ORDER):
            out_ref[s, :, 48 * t : 48 * t + 48] = w_ref[tap, :, 48 * s : 48 * s + 48]


def attention_kernel(
    flag_ref, own_ref, back_ref, mod_ref, a0, b0, a1, b1, a2, b2, a3, b3, o0, o1, o2, o3, heads, w_out, total_out
):
    first = flag_ref[0] > 0
    scale = 1.0 / math.sqrt(HEAD_DIM)
    shift, gain = mod_ref[0:1, :], mod_ref[1:2, :]
    own = norm_rows(own_ref[...], shift, gain).astype(bf16)
    back = norm_rows(back_ref[...], shift, gain).astype(bf16)
    for h, (wa, wb) in enumerate(((a0, b0), (a1, b1), (a2, b2), (a3, b3))):
        qk = mm_t(own, wa[0:128, :]).astype(bf16)
        q, k = qk[:, 0:64], qk[:, 64:128]
        v = mm_t(own, wb[0:64, :]).astype(bf16)
        kb = mm_t(back, wa[64:128, :]).astype(bf16)
        vb = mm_t(back, wb[0:64, :]).astype(bf16)
        s_own = mm_t(q, k) * scale
        s_back = mm_t(q, kb) * scale
        s_back = jnp.where(first, -1e30, s_back)
        top = jnp.maximum(
            jnp.max(s_own, axis=-1, keepdims=True), jnp.max(s_back, axis=-1, keepdims=True)
        )
        e_own = jnp.exp(s_own - top)
        e_back = jnp.exp(s_back - top)
        total = jnp.sum(e_own, axis=-1, keepdims=True) + jnp.sum(e_back, axis=-1, keepdims=True)
        inv = 1.0 / total
        p_own = (e_own * inv).astype(bf16)
        p_back = (e_back * inv).astype(bf16)
        heads[:, 64 * h : 64 * h + 64] = (mm(p_own, v) + mm(p_back, vb)).astype(bf16)
        w_out[64 * h : 64 * h + 64, :] = wb[64:128, :]
    total_out[...] = mm(heads[...], w_out[...]).astype(bf16)
    for k, out in enumerate((o0, o1, o2, o3)):
        start = pl.multiple_of(64 * (flag_ref[1] ^ k), 64)
        out[...] = total_out[pl.ds(start, 64), :]


def sum_of(p0, p1, p2, p3):
    return (p0[...].astype(f32) + p1[...].astype(f32)) + (p2[...].astype(f32) + p3[...].astype(f32))


def after_attention_kernel(p0, p1, p2, p3, frames_ref, mod_ref, mixed_ref, norm_ref):
    attn = sum_of(p0, p1, p2, p3)
    mixed = (frames_ref[...].astype(f32) + mod_ref[2:3, :] * attn).astype(bf16)
    mixed_ref[...] = mixed
    norm_ref[...] = norm_rows(mixed, mod_ref[3:4, :], mod_ref[4:5, :]).astype(bf16)


def mlp_kernel(h0, h1, h2, h3, w0, w1, w2, w3, o0, o1, o2, o3, acc):
    h = jnp.concatenate([h0[...], h1[...], h2[...], h3[...]], axis=0)
    for i, w in enumerate((w0, w1, w2, w3)):
        up = mm(h, w[0:1024, :])
        hid = jax.nn.gelu(up, approximate=True).astype(bf16)
        for k in range(4):
            part = mm(hid, w[1024 + 256 * k : 1280 + 256 * k, :])
            cols = slice(256 * k, 256 * k + 256)
            if i == 0:
                acc[:, cols] = part
            elif i < 3:
                acc[:, cols] += part
            else:
                value = (acc[:, cols] + part).astype(bf16)
                for n, out in enumerate((o0, o1, o2, o3)):
                    out[:, cols] = value[64 * n : 64 * n + 64]


def after_mlp_kernel(p0, p1, p2, p3, mixed_ref, mod_ref, wv_ref, noisy_ref, out_ref):
    feed = sum_of(p0, p1, p2, p3)
    final = (mixed_ref[...].astype(f32) + mod_ref[5:6, :] * feed).astype(bf16)
    normed = norm_rows(final, mod_ref[6:7, :], mod_ref[7:8, :]).astype(bf16)
    mel = noisy_ref[...] + 0.5 * mm(normed, wv_ref[...])
    for s in range(16):
        out_ref[s] = mel


def placed_kernel(comp_ref, full_ref, here_ref):
    earlier = lax.broadcasted_iota(jnp.int32, (100, 192), 1) < 96
    full_ref[...] = jnp.zeros(full_ref.shape, bf16)
    here_ref[...] = jnp.zeros(here_ref.shape, bf16)
    here = [comp_ref[100 * j : 100 * j + 100, 0:192] for j in range(7)]
    near = [comp_ref[100 * j : 100 * j + 100, 192:384] for j in range(7)]
    for d in range(OFFSETS):
        value = jnp.zeros((100, 192), f32)
        if 0 <= d - 1 < 7:
            value = here[d - 1]
            here_ref[MEL_PAD * d : MEL_PAD * d + 100, :] = value.astype(bf16)
        if d < 7:
            value = value + jnp.where(earlier, near[d], 0.0)
        if 0 <= d - 2 < 7:
            value = value + jnp.where(earlier, 0.0, near[d - 2])
        full_ref[MEL_PAD * d : MEL_PAD * d + 100, :] = value.astype(bf16)


EXT = 1056


def upsample_kernel(flag_ref, mel_ref, before_ref, after_ref, full_ref, here_ref, out_ref, ext, up):
    ext[...] = jnp.zeros((EXT, MEL_PAD), f32)
    ext[0:8, 0:100] = before_ref[...]
    for s in range(16):
        ext[8 + 64 * s : 72 + 64 * s, 0:100] = mel_ref[s]
    ext[1032:1040, 0:100] = after_ref[...]
    cols = [ext[3 + k : 3 + k + 1032, :].astype(bf16) for k in range(OFFSETS)]
    up[...] = mm(jnp.concatenate(cols, axis=1), full_ref[...])
    earlier = lax.broadcasted_iota(jnp.int32, (8, 192), 1) < 96
    row = lax.broadcasted_iota(jnp.int32, (8, 192), 0)
    for which, base, r in ((0, 0, 1), (1, 1024, 0)):
        edge_cols = [ext[base + 3 + k : base + 11 + k, :].astype(bf16) for k in range(OFFSETS)]
        edge = mm(jnp.concatenate(edge_cols, axis=1), here_ref[...])
        lanes = earlier if which == 0 else jnp.logical_not(earlier)
        use = (flag_ref[which] > 0) & (row == r) & lanes
        up[base : base + 8, :] = jnp.where(use, edge, up[base : base + 8, :])
    for s in range(16):
        out_ref[s] = up[64 * s : 64 * s + ROWS, :].astype(bf16)


PI_PARTS = (3.140625, 0.000965118408203125, 2.5331974029541016e-06, 1.984187258941006e-09)


def sin_squared(x):
    k = jnp.round(x * (1.0 / math.pi))
    r = x
    for part in PI_PARTS:
        r = r - k * part
    z = r * r
    poly = -2.3889859e-08 * z + 2.7525562e-06
    poly = poly * z - 1.9840874e-04
    poly = poly * z + 8.3333310e-03
    poly = poly * z - 1.6666667e-01
    sine = r + r * (z * poly)
    return sine * sine


def snake_act(values, alpha_row, inverse_row):
    return values + sin_squared(alpha_row * values) * inverse_row


def shifted(plane, by):
    return pltpu.roll(plane, by % plane.shape[0], 0)


ROWS = 72


def conv_weights_kernel(w_hbm, out_ref, sem):
    copy = pltpu.make_async_copy(w_hbm.at[:, pl.ds(96, 288), :], out_ref, sem)
    copy.start()
    copy.wait()


def conv_kernel(flag_ref, up_ref, alpha_ref, w_ref, out_ref, planes):
    first = flag_ref[0] > 0
    last = flag_ref[1] > 0
    row = lax.broadcasted_iota(jnp.int32, (ROWS, 768), 0)
    outside = (first & (row == 0)) | (last & (row == 65))
    for s in range(16):
        for p in range(4):
            planes[p, :, 48 * s : 48 * s + 48] = up_ref[s, :, 48 * p : 48 * p + 48]
    a1 = alpha_ref[0:1, :]
    a2 = alpha_ref[1:2, :]
    i1 = 1.0 / a1
    i2 = 1.0 / a2

    def weight(base, tap):
        return jnp.concatenate(
            [w_ref[s, base + 48 * tap : base + 48 * tap + 48, :] for s in range(16)], axis=0
        )

    ups = []
    acts = []
    for p in range(4):
        u = jnp.where(outside, 0.0, planes[p].astype(f32))
        ups.append(u)
        acts.append(snake_act(u, a1, i1).astype(bf16))
    act = jnp.concatenate(acts, axis=0)
    y = [mm(act, weight(0, tap)) for tap in range(3)]
    y = [[v[ROWS * p : ROWS * p + ROWS] for p in range(4)] for v in y]
    acts = []
    for p in range(4):
        before = y[0][0] if p == 3 else shifted(y[0][p + 1], 1)
        after = y[2][3] if p == 0 else shifted(y[2][p - 1], -1)
        inner = before + y[1][p] + after
        acts.append(jnp.where(outside, 0.0, snake_act(inner, a2, i2)).astype(bf16))
    act = jnp.concatenate(acts, axis=0)
    y = [mm(act, weight(144, tap)) for tap in range(3)]
    y = [[v[ROWS * p : ROWS * p + ROWS] for p in range(4)] for v in y]
    for p in range(4):
        before = y[0][p - 1] if p >= 1 else shifted(y[0][3], 1)
        after = y[2][p + 1] if p <= 2 else shifted(y[2][0], -1)
        total = ups[p] + (before + y[1][p] + after)
        out_ref[:, 768 * p : 768 * p + 768] = shifted(total, -1)[0:64].astype(bf16)


def gather(value, groups):
    return lax.all_gather(value, "sub", axis=0, tiled=True, axis_index_groups=groups)


def exchange(value, groups=None, axis="sub"):
    return lax.all_to_all(value, axis, 0, 0, tiled=True, axis_index_groups=groups)


def device(y_hi, z, x, y_lo, core):
    return (y_hi * 8 + z) * 16 + x * 4 + y_lo * 2 + core


OTHER_Y = [
    (device(h, z, x, y, c), device(1 - h, z, x, 1 - y, c))
    for h in range(2)
    for z in range(8)
    for x in range(4)
    for y in range(2)
    for c in range(2)
]
OTHER_GROUPS = [
    [device(y ^ side, z, x, y, c) for x in range(4) for y in range(2) for c in range(2)]
    for side in range(2)
    for z in range(8)
]


def program(
    frames,
    modulation,
    w_project,
    w_heads_out,
    w_up,
    w_down,
    w_velocity,
    noisy_mel,
    w_prelude,
    w_upsample,
    snake_alpha,
    w_dilated,
    w_plain,
):
    own_rows = frames.shape[0]
    sub_index = lax.axis_index("sub")
    time_index = lax.axis_index("tm")
    n_sub = lax.axis_size("sub")
    n_tm = lax.axis_size("tm")
    n_all = n_sub * n_tm
    both = ("tm", "sub")
    shape = jax.ShapeDtypeStruct
    here_index = time_index * n_sub + sub_index

    to_right = [(i, (i + 4) % 16) for i in range(16)]
    to_left = [(i, (i - 4) % 16) for i in range(16)]
    own_a, own_b, w_voc = whole(
        first_weights_kernel,
        (shape((128, 1024), bf16), shape((128, 1024), bf16), shape((384, 768), bf16)),
        (jnp.swapaxes(w_project, 1, 2), w_heads_out, w_prelude, w_dilated, w_plain),
        cost=cost_of(0, 3 << 20),
    )
    back_frames = lax.ppermute(frames, both, [(i, i + 4) for i in range(n_all - 4)])
    left_a = lax.ppermute(own_a, "sub", to_right)
    right_b = lax.ppermute(own_b, "sub", to_left)
    left_b = lax.ppermute(own_b, "sub", to_right)
    right_a = lax.ppermute(own_a, "sub", to_left)
    far_a = lax.ppermute(left_a, "sub", to_right)
    far_b = lax.ppermute(right_b, "sub", to_left)

    w_voc = lax.all_gather(w_voc, "sub", axis=0, tiled=False)

    block = gather(frames, J_GROUPS)
    back = gather(back_frames, J_GROUPS)

    own_mlp = whole(
        mlp_weights_kernel, shape((2048, 256), bf16), (w_up, w_down), cost=cost_of(0, 2 << 20)
    )
    other_core = lax.ppermute(own_mlp, "sub", [(i, i ^ 1) for i in range(16)])
    other_y = lax.ppermute(own_mlp, both, OTHER_Y)
    other_both = lax.ppermute(other_y, "sub", [(i, i ^ 1) for i in range(16)])

    ups = whole(
        upsample_weights_kernel, shape((16, 96, 384), bf16), (w_upsample,), cost=cost_of(0, 3 << 20)
    )

    is_first = (time_index == 0) & (sub_index < 4)
    quarter = shape((own_rows, 1024), bf16)
    partial = whole(
        attention_kernel,
        (quarter,) * 4,
        (
            jnp.stack([is_first.astype(jnp.int32), lax.rem(sub_index, 4)]),
            block,
            back,
            modulation,
            own_a,
            own_b,
            left_a,
            left_b,
            right_a,
            right_b,
            far_a,
            far_b,
        ),
        scratch=[pltpu.VMEM((BLK, 256), bf16)] + [pltpu.VMEM((256, 1024), bf16)] * 2,
        cost=cost_of(10**9, 4 << 20, 1 << 19),
        smem=1,
    )
    ups = exchange(ups, OTHER_GROUPS, both)
    parts = [partial[0]] + [
        lax.ppermute(partial[k], "sub", [(i, i ^ k) for i in range(16)]) for k in (1, 2, 3)
    ]
    mixed_rows, own_norm = whole(
        after_attention_kernel,
        (quarter, quarter),
        (*parts, frames, modulation),
        cost=cost_of(10**6, 1 << 20),
    )

    own_norm, ups = lax.optimization_barrier((own_norm, ups))
    across = [(i, (i + 8) % 16) for i in range(16)]
    second = [
        own_norm,
        lax.ppermute(own_norm, "sub", across),
        lax.ppermute(own_norm, "sub", to_right),
        lax.ppermute(own_norm, "sub", to_left),
    ]
    partial = whole(
        mlp_kernel,
        (quarter,) * 4,
        (*second, own_mlp, other_core, other_y, other_both),
        scratch=[pltpu.VMEM((256, 1024), f32)],
        cost=cost_of(11 * 10**8, 5 << 20, 1 << 18),
    )
    parts = [
        partial[0],
        lax.ppermute(partial[1], "sub", across),
        lax.ppermute(partial[2], "sub", to_left),
        lax.ppermute(partial[3], "sub", to_right),
    ]
    noisy_own = lax.dynamic_slice_in_dim(noisy_mel, sub_index * own_rows, own_rows, 0)
    copies = whole(
        after_mlp_kernel,
        shape((16, own_rows, 100), f32),
        (*parts, mixed_rows, modulation, w_velocity, noisy_own),
        cost=cost_of(10**7, 1 << 20),
    )
    mel_all = exchange(copies)
    mel_next = mel_all.reshape(-1, 100)

    pre_all = w_voc[:, :96, :].reshape(1536, 768)
    comp = lax.dot_general(
        pre_all, ups.reshape(1536, 384), (((0,), (0,)), ((), ())), preferred_element_type=f32
    )
    w_full, w_here = whole(
        placed_kernel,
        (shape((OFFSETS * MEL_PAD, 192), bf16), shape((OFFSETS * MEL_PAD, 192), bf16)),
        (comp,),
        cost=cost_of(10**6, 2 << 20),
    )

    before = lax.ppermute(mel_all[15, 56:], "tm", [(i, i + 1) for i in range(n_tm - 1)])
    after = lax.ppermute(mel_all[0, :8], "tm", [(i + 1, i) for i in range(n_tm - 1)])
    windows = whole(
        upsample_kernel,
        shape((16, ROWS, 192), bf16),
        (
            jnp.stack([time_index == 0, time_index == n_tm - 1]).astype(jnp.int32),
            mel_all,
            before,
            after,
            w_full,
            w_here,
        ),
        scratch=[pltpu.VMEM((EXT, MEL_PAD), f32), pltpu.VMEM((1032, 192), f32)],
        cost=cost_of(5 * 10**8, 2 << 20),
        smem=1,
    )
    up_x = exchange(windows)

    flags = jnp.stack([here_index == 0, here_index == n_all - 1]).astype(jnp.int32)
    w_conv = pl.pallas_call(
        conv_weights_kernel,
        out_shape=shape((16, 288, 768), bf16),
        in_specs=[pl.BlockSpec(memory_space=pl.ANY)],
        out_specs=pl.BlockSpec(memory_space=pltpu.VMEM),
        scratch_shapes=[pltpu.SemaphoreType.DMA],
        compiler_params=pltpu.CompilerParams(vmem_limit_bytes=16 << 20),
        cost_estimate=cost_of(0, 14 << 20),
        name="conv_weights",
    )(w_voc)
    out = whole(
        conv_kernel,
        shape((64, 3072), bf16),
        (flags, up_x, snake_alpha, w_conv),
        scratch=[pltpu.VMEM((4, ROWS, 768), bf16)],
        cost=cost_of(2 * 10**9, 8 << 20, 1 << 18),
        smem=1,
        vmem=32,
    )
    return (mel_next, out.reshape(256, 768))


def solution(mesh):
    in_specs = (
        P(("tm", "sub"), None),
        P(),
        P(None, None, "sub"),
        P("sub", None),
        P(None, "sub"),
        P("sub", None),
        P(),
        P("tm", None),
        P(None, "sub", None),
        P(None, "sub", None),
        P(),
        P(None, "sub", None),
        P(None, "sub", None),
    )
    out_specs = (P("tm", None), P(("tm", "sub"), None))
    return jax.shard_map(program, mesh=mesh, in_specs=in_specs, out_specs=out_specs, check_vma=False)
```

```python
import math

import jax
import jax.numpy as jnp
from jax import lax
from jax.experimental import pallas as pl
from jax.experimental.pallas import tpu as pltpu
from jax.sharding import PartitionSpec as P


HEAD_DIM = 64
BLK = 256
MEL_PAD = 128
OFFSETS = 9

epsilon = 1e-06
bf16 = jnp.bfloat16
f32 = jnp.float32


def norm_rows(rows, offset_row, scale_row):
    rows = rows.astype(f32)
    center = jnp.mean(rows, axis=-1, keepdims=True)
    square = jnp.mean(rows * rows, axis=-1, keepdims=True)
    spread = square - center * center
    return (rows - center) * lax.rsqrt(spread + epsilon) * (1.0 + scale_row) + offset_row


def mm(a, b):
    return jnp.dot(a, b, preferred_element_type=f32)


def mm_t(a, b):
    return lax.dot_general(a, b, (((1,), (1,)), ((), ())), preferred_element_type=f32)


def vmem_specs(n):
    return [pl.BlockSpec(memory_space=pltpu.VMEM)] * n


def whole(kernel, out_shapes, args, scratch=(), cost=None, smem=0, vmem=24):
    single = not isinstance(out_shapes, (tuple, list))
    return pl.pallas_call(
        kernel,
        out_shape=out_shapes,
        in_specs=[pl.BlockSpec(memory_space=pltpu.SMEM)] * smem + vmem_specs(len(args) - smem),
        out_specs=vmem_specs(1)[0] if single else vmem_specs(len(out_shapes)),
        scratch_shapes=list(scratch),
        compiler_params=pltpu.CompilerParams(vmem_limit_bytes=vmem << 20),
        cost_estimate=cost,
    )(*args)


def cost_of(flops, nbytes, trans=0):
    return pl.CostEstimate(flops=flops, bytes_accessed=nbytes, transcendentals=trans)


def first_weights_kernel(
    w_ref, o_ref, pre_ref, dil_ref, plain_ref, a_ref, b_ref, voc_ref, pre_scratch, sems
):
    moves = (
        (w_ref.at[0], a_ref.at[pl.ds(0, 64), :]),
        (w_ref.at[1], a_ref.at[pl.ds(64, 64), :]),
        (w_ref.at[2], b_ref.at[pl.ds(0, 64), :]),
        (o_ref, b_ref.at[pl.ds(64, 64), :]),
        (dil_ref, voc_ref.at[pl.ds(96, 144), :]),
        (plain_ref, voc_ref.at[pl.ds(240, 144), :]),
        (pre_ref, pre_scratch),
    )
    copies = [pltpu.make_async_copy(src, dst, sems.at[n]) for n, (src, dst) in enumerate(moves)]
    for copy in copies:
        copy.start()
    voc_ref[0:96, :] = jnp.zeros((96, 768), bf16)
    copies[6].wait()
    for k in range(7):
        voc_ref[0:96, 100 * k : 100 * k + 100] = pre_scratch[k]
    for copy in copies[:6]:
        copy.wait()


def mlp_weights_kernel(up_ref, down_ref, out_ref):
    out_ref[0:1024, :] = up_ref[...]
    for k in range(4):
        out_ref[1024 + 256 * k : 1280 + 256 * k, :] = down_ref[:, 256 * k : 256 * k + 256]


TAP_ORDER = (2, 3, 4, 5, 6, 7, 0, 1)


def upsample_weights_kernel(w_ref, out_ref):
    for s in range(16):
        for t, tap in enumerate(TAP_ORDER):
            out_ref[s, :, 48 * t : 48 * t + 48] = w_ref[tap, :, 48 * s : 48 * s + 48]


def attention_kernel(flag_ref, mod_ref, *refs):
    row_refs, weight_refs = refs[:8], refs[8:16]
    o0, o1, o2, o3, rows, w_a, w_v, w_out, heads, sems = refs[16:]
    copies = []
    for n, ref in enumerate(row_refs):
        copies.append((ref, rows.at[pl.ds(64 * n, 64), :]))
    for h in range(4):
        first_half, second_half = weight_refs[2 * h], weight_refs[2 * h + 1]
        copies.append((first_half, w_a.at[h]))
        copies.append((second_half.at[pl.ds(0, 64), :], w_v.at[h]))
        copies.append((second_half.at[pl.ds(64, 64), :], w_out.at[pl.ds(64 * h, 64), :]))
    copies = [pltpu.make_async_copy(src, dst, sems.at[n]) for n, (src, dst) in enumerate(copies)]
    for copy in copies:
        copy.start()
    first = flag_ref[0] > 0
    scale = 1.0 / math.sqrt(HEAD_DIM)
    for copy in copies[:8]:
        copy.wait()
    normed = norm_rows(rows[...], mod_ref[0:1, :], mod_ref[1:2, :]).astype(bf16)
    own, back = normed[:BLK], normed[BLK:]
    for copy in copies[8:]:
        copy.wait()
    for h in range(4):
        qk = mm_t(own, w_a[h]).astype(bf16)
        q, k = qk[:, 0:64], qk[:, 64:128]
        v = mm_t(own, w_v[h]).astype(bf16)
        kb = mm_t(back, w_a[h, 64:128, :]).astype(bf16)
        vb = mm_t(back, w_v[h]).astype(bf16)
        s_own = mm_t(q, k) * scale
        s_back = mm_t(q, kb) * scale
        s_back = jnp.where(first, -1e30, s_back)
        top = jnp.maximum(
            jnp.max(s_own, axis=-1, keepdims=True), jnp.max(s_back, axis=-1, keepdims=True)
        )
        e_own = jnp.exp(s_own - top)
        e_back = jnp.exp(s_back - top)
        total = jnp.sum(e_own, axis=-1, keepdims=True) + jnp.sum(e_back, axis=-1, keepdims=True)
        inv = 1.0 / total
        p_own = (e_own * inv).astype(bf16)
        p_back = (e_back * inv).astype(bf16)
        heads[:, 64 * h : 64 * h + 64] = (mm(p_own, v) + mm(p_back, vb)).astype(bf16)
    total = mm(heads[...], w_out[...]).astype(bf16)
    for k, out in enumerate((o0, o1, o2, o3)):
        out[...] = total[64 * k : 64 * k + 64]


def sum_of(p0, p1, p2, p3):
    return (p0[...].astype(f32) + p1[...].astype(f32)) + (p2[...].astype(f32) + p3[...].astype(f32))


def after_attention_kernel(p0, p1, p2, p3, frames_ref, mod_ref, mixed_ref, norm_ref):
    attn = sum_of(p0, p1, p2, p3)
    mixed = (frames_ref[...].astype(f32) + mod_ref[2:3, :] * attn).astype(bf16)
    mixed_ref[...] = mixed
    norm_ref[...] = norm_rows(mixed, mod_ref[3:4, :], mod_ref[4:5, :]).astype(bf16)


def mlp_kernel(h0, h1, h2, h3, w0, w1, w2, w3, o0, o1, o2, o3, acc):
    h = jnp.concatenate([h0[...], h1[...], h2[...], h3[...]], axis=0)
    for i, w in enumerate((w0, w1, w2, w3)):
        up = mm(h, w[0:1024, :])
        hid = jax.nn.gelu(up, approximate=True).astype(bf16)
        for k in range(4):
            part = mm(hid, w[1024 + 256 * k : 1280 + 256 * k, :])
            cols = slice(256 * k, 256 * k + 256)
            if i == 0:
                acc[:, cols] = part
            elif i < 3:
                acc[:, cols] += part
            else:
                value = (acc[:, cols] + part).astype(bf16)
                for n, out in enumerate((o0, o1, o2, o3)):
                    out[:, cols] = value[64 * n : 64 * n + 64]


def after_mlp_kernel(p0, p1, p2, p3, mixed_ref, mod_ref, wv_ref, noisy_ref, out_ref):
    feed = sum_of(p0, p1, p2, p3)
    final = (mixed_ref[...].astype(f32) + mod_ref[5:6, :] * feed).astype(bf16)
    normed = norm_rows(final, mod_ref[6:7, :], mod_ref[7:8, :]).astype(bf16)
    mel = noisy_ref[...] + 0.5 * mm(normed, wv_ref[...])
    for s in range(16):
        out_ref[s] = mel


def placed_kernel(comp_ref, full_ref, here_ref):
    earlier = lax.broadcasted_iota(jnp.int32, (100, 192), 1) < 96
    full_ref[...] = jnp.zeros(full_ref.shape, bf16)
    here_ref[...] = jnp.zeros(here_ref.shape, bf16)
    here = [comp_ref[100 * j : 100 * j + 100, 0:192] for j in range(7)]
    near = [comp_ref[100 * j : 100 * j + 100, 192:384] for j in range(7)]
    for d in range(OFFSETS):
        value = jnp.zeros((100, 192), f32)
        if 0 <= d - 1 < 7:
            value = here[d - 1]
            here_ref[MEL_PAD * d : MEL_PAD * d + 100, :] = value.astype(bf16)
        if d < 7:
            value = value + jnp.where(earlier, near[d], 0.0)
        if 0 <= d - 2 < 7:
            value = value + jnp.where(earlier, 0.0, near[d - 2])
        full_ref[MEL_PAD * d : MEL_PAD * d + 100, :] = value.astype(bf16)


EXT = 1056


def upsample_kernel(flag_ref, mel_ref, before_ref, after_ref, full_ref, here_ref, out_ref, ext, up):
    ext[...] = jnp.zeros((EXT, MEL_PAD), f32)
    ext[0:8, 0:100] = before_ref[...]
    for s in range(16):
        ext[8 + 64 * s : 72 + 64 * s, 0:100] = mel_ref[s]
    ext[1032:1040, 0:100] = after_ref[...]
    cols = [ext[3 + k : 3 + k + 1032, :].astype(bf16) for k in range(OFFSETS)]
    up[...] = mm(jnp.concatenate(cols, axis=1), full_ref[...])
    earlier = lax.broadcasted_iota(jnp.int32, (8, 192), 1) < 96
    row = lax.broadcasted_iota(jnp.int32, (8, 192), 0)
    for which, base, r in ((0, 0, 1), (1, 1024, 0)):
        edge_cols = [ext[base + 3 + k : base + 11 + k, :].astype(bf16) for k in range(OFFSETS)]
        edge = mm(jnp.concatenate(edge_cols, axis=1), here_ref[...])
        lanes = earlier if which == 0 else jnp.logical_not(earlier)
        use = (flag_ref[which] > 0) & (row == r) & lanes
        up[base : base + 8, :] = jnp.where(use, edge, up[base : base + 8, :])
    for s in range(16):
        out_ref[s] = up[64 * s : 64 * s + ROWS, :].astype(bf16)


PI_PARTS = (3.140625, 0.000965118408203125, 2.5331974029541016e-06, 1.984187258941006e-09)


def sin_squared(x):
    k = jnp.round(x * (1.0 / math.pi))
    r = x
    for part in PI_PARTS:
        r = r - k * part
    z = r * r
    poly = -2.3889859e-08 * z + 2.7525562e-06
    poly = poly * z - 1.9840874e-04
    poly = poly * z + 8.3333310e-03
    poly = poly * z - 1.6666667e-01
    sine = r + r * (z * poly)
    return sine * sine


def snake_act(values, alpha_row, inverse_row):
    return values + sin_squared(alpha_row * values) * inverse_row


def shifted(plane, by):
    return pltpu.roll(plane, by % plane.shape[0], 0)


ROWS = 72


def conv_weights_kernel(w_hbm, out_ref, sem):
    copy = pltpu.make_async_copy(w_hbm.at[:, pl.ds(96, 288), :], out_ref, sem)
    copy.start()
    copy.wait()


def conv_kernel(flag_ref, up_ref, alpha_ref, w_ref, out_ref, planes):
    first = flag_ref[0] > 0
    last = flag_ref[1] > 0
    row = lax.broadcasted_iota(jnp.int32, (ROWS, 768), 0)
    outside = (first & (row == 0)) | (last & (row == 65))
    for s in range(16):
        for p in range(4):
            planes[p, :, 48 * s : 48 * s + 48] = up_ref[s, :, 48 * p : 48 * p + 48]
    a1 = alpha_ref[0:1, :]
    a2 = alpha_ref[1:2, :]
    i1 = 1.0 / a1
    i2 = 1.0 / a2

    def weight(base, tap):
        return jnp.concatenate(
            [w_ref[s, base + 48 * tap : base + 48 * tap + 48, :] for s in range(16)], axis=0
        )

    ups = []
    acts = []
    for p in range(4):
        u = jnp.where(outside, 0.0, planes[p].astype(f32))
        ups.append(u)
        acts.append(snake_act(u, a1, i1).astype(bf16))
    act = jnp.concatenate(acts, axis=0)
    y = [mm(act, weight(0, tap)) for tap in range(3)]
    y = [[v[ROWS * p : ROWS * p + ROWS] for p in range(4)] for v in y]
    acts = []
    for p in range(4):
        before = y[0][0] if p == 3 else shifted(y[0][p + 1], 1)
        after = y[2][3] if p == 0 else shifted(y[2][p - 1], -1)
        inner = before + y[1][p] + after
        acts.append(jnp.where(outside, 0.0, snake_act(inner, a2, i2)).astype(bf16))
    act = jnp.concatenate(acts, axis=0)
    y = [mm(act, weight(144, tap)) for tap in range(3)]
    y = [[v[ROWS * p : ROWS * p + ROWS] for p in range(4)] for v in y]
    for p in range(4):
        before = y[0][p - 1] if p >= 1 else shifted(y[0][3], 1)
        after = y[2][p + 1] if p <= 2 else shifted(y[2][0], -1)
        total = ups[p] + (before + y[1][p] + after)
        out_ref[:, 768 * p : 768 * p + 768] = shifted(total, -1)[0:64].astype(bf16)


def exchange(value, groups=None, axis="sub"):
    return lax.all_to_all(value, axis, 0, 0, tiled=True, axis_index_groups=groups)


def device(y_hi, z, x, y_lo, core):
    return (y_hi * 8 + z) * 16 + x * 4 + y_lo * 2 + core


OTHER_Y = [
    (device(h, z, x, y, c), device(1 - h, z, x, 1 - y, c))
    for h in range(2)
    for z in range(8)
    for x in range(4)
    for y in range(2)
    for c in range(2)
]
OTHER_GROUPS = [
    [device(y ^ side, z, x, y, c) for x in range(4) for y in range(2) for c in range(2)]
    for side in range(2)
    for z in range(8)
]


def program(
    frames,
    modulation,
    w_project,
    w_heads_out,
    w_up,
    w_down,
    w_velocity,
    noisy_mel,
    w_prelude,
    w_upsample,
    snake_alpha,
    w_dilated,
    w_plain,
):
    own_rows = frames.shape[0]
    sub_index = lax.axis_index("sub")
    time_index = lax.axis_index("tm")
    n_sub = lax.axis_size("sub")
    n_tm = lax.axis_size("tm")
    n_all = n_sub * n_tm
    both = ("tm", "sub")
    shape = jax.ShapeDtypeStruct
    here_index = time_index * n_sub + sub_index

    to_right = [(i, (i + 4) % 16) for i in range(16)]
    to_left = [(i, (i - 4) % 16) for i in range(16)]
    own_a, own_b, w_voc = pl.pallas_call(
        first_weights_kernel,
        out_shape=(shape((128, 1024), bf16), shape((128, 1024), bf16), shape((384, 768), bf16)),
        in_specs=[pl.BlockSpec(memory_space=pl.ANY)] * 5,
        out_specs=vmem_specs(3),
        scratch_shapes=[pltpu.VMEM((7, 96, 100), bf16), pltpu.SemaphoreType.DMA((7,))],
        compiler_params=pltpu.CompilerParams(vmem_limit_bytes=60 << 20),
        cost_estimate=cost_of(0, 3 << 20),
        name="first_weights",
    )(
        jnp.swapaxes(w_project, 1, 2),
        w_heads_out,
        w_prelude,
        w_dilated.reshape(144, 768),
        w_plain.reshape(144, 768),
    )
    back_frames = lax.ppermute(frames, both, [(i, i + 4) for i in range(n_all - 4)])
    left_a = lax.ppermute(own_a, "sub", to_right)
    right_b = lax.ppermute(own_b, "sub", to_left)
    left_b = lax.ppermute(own_b, "sub", to_right)
    right_a = lax.ppermute(own_a, "sub", to_left)
    far_a = lax.ppermute(left_a, "sub", to_right)
    far_b = lax.ppermute(right_b, "sub", to_left)

    w_voc = lax.all_gather(w_voc, "sub", axis=0, tiled=False)

    beside = [[(i, i ^ k) for i in range(16)] for k in (1, 2, 3)]
    block = [frames] + [lax.ppermute(frames, "sub", beside[k - 1]) for k in (1, 2, 3)]
    back = [back_frames] + [lax.ppermute(back_frames, "sub", beside[k - 1]) for k in (1, 2, 3)]

    own_mlp = whole(
        mlp_weights_kernel, shape((2048, 256), bf16), (w_up, w_down), cost=cost_of(0, 2 << 20)
    )
    other_core = lax.ppermute(own_mlp, "sub", [(i, i ^ 1) for i in range(16)])
    other_y = lax.ppermute(own_mlp, both, OTHER_Y)
    other_both = lax.ppermute(other_y, "sub", [(i, i ^ 1) for i in range(16)])

    ups = whole(
        upsample_weights_kernel, shape((16, 96, 384), bf16), (w_upsample,), cost=cost_of(0, 3 << 20)
    )

    is_first = (time_index == 0) & (sub_index < 4)
    quarter = shape((own_rows, 1024), bf16)
    partial = pl.pallas_call(
        attention_kernel,
        out_shape=(quarter,) * 4,
        in_specs=[pl.BlockSpec(memory_space=pltpu.SMEM)]
        + vmem_specs(1)
        + [pl.BlockSpec(memory_space=pl.ANY)] * 16,
        out_specs=vmem_specs(4),
        scratch_shapes=[
            pltpu.VMEM((2 * BLK, 1024), bf16),
            pltpu.VMEM((4, 128, 1024), bf16),
            pltpu.VMEM((4, 64, 1024), bf16),
            pltpu.VMEM((256, 1024), bf16),
            pltpu.VMEM((BLK, 256), bf16),
            pltpu.SemaphoreType.DMA((20,)),
        ],
        compiler_params=pltpu.CompilerParams(vmem_limit_bytes=60 << 20),
        cost_estimate=cost_of(10**9, 4 << 20, 1 << 19),
        name="attention",
    )(
        is_first.astype(jnp.int32).reshape(1),
        modulation,
        *block,
        *back,
        own_a,
        own_b,
        left_a,
        left_b,
        right_a,
        right_b,
        far_a,
        far_b,
    )
    ups = exchange(ups, OTHER_GROUPS, both)
    parts = [partial[0]] + [lax.ppermute(partial[k], "sub", beside[k - 1]) for k in (1, 2, 3)]
    mixed_rows, own_norm = whole(
        after_attention_kernel,
        (quarter, quarter),
        (*parts, frames, modulation),
        cost=cost_of(10**6, 1 << 20),
    )

    own_norm, ups = lax.optimization_barrier((own_norm, ups))
    across = [(i, (i + 8) % 16) for i in range(16)]
    second = [
        own_norm,
        lax.ppermute(own_norm, "sub", across),
        lax.ppermute(own_norm, "sub", to_right),
        lax.ppermute(own_norm, "sub", to_left),
    ]
    partial = whole(
        mlp_kernel,
        (quarter,) * 4,
        (*second, own_mlp, other_core, other_y, other_both),
        scratch=[pltpu.VMEM((256, 1024), f32)],
        cost=cost_of(11 * 10**8, 5 << 20, 1 << 18),
    )
    parts = [
        partial[0],
        lax.ppermute(partial[1], "sub", across),
        lax.ppermute(partial[2], "sub", to_left),
        lax.ppermute(partial[3], "sub", to_right),
    ]
    noisy_own = lax.dynamic_slice_in_dim(noisy_mel, sub_index * own_rows, own_rows, 0)
    copies = whole(
        after_mlp_kernel,
        shape((16, own_rows, 100), f32),
        (*parts, mixed_rows, modulation, w_velocity, noisy_own),
        cost=cost_of(10**7, 1 << 20),
    )
    mel_all = exchange(copies)
    mel_next = mel_all.reshape(-1, 100)

    pre_all = w_voc[:, :96, :].reshape(1536, 768)
    comp = lax.dot_general(
        pre_all, ups.reshape(1536, 384), (((0,), (0,)), ((), ())), preferred_element_type=f32
    )
    w_full, w_here = whole(
        placed_kernel,
        (shape((OFFSETS * MEL_PAD, 192), bf16), shape((OFFSETS * MEL_PAD, 192), bf16)),
        (comp,),
        cost=cost_of(10**6, 2 << 20),
    )

    before = lax.ppermute(mel_all[15, 56:], "tm", [(i, i + 1) for i in range(n_tm - 1)])
    after = lax.ppermute(mel_all[0, :8], "tm", [(i + 1, i) for i in range(n_tm - 1)])
    windows = whole(
        upsample_kernel,
        shape((16, ROWS, 192), bf16),
        (
            jnp.stack([time_index == 0, time_index == n_tm - 1]).astype(jnp.int32),
            mel_all,
            before,
            after,
            w_full,
            w_here,
        ),
        scratch=[pltpu.VMEM((EXT, MEL_PAD), f32), pltpu.VMEM((1032, 192), f32)],
        cost=cost_of(5 * 10**8, 2 << 20),
        smem=1,
    )
    up_x = exchange(windows)

    flags = jnp.stack([here_index == 0, here_index == n_all - 1]).astype(jnp.int32)
    w_conv = pl.pallas_call(
        conv_weights_kernel,
        out_shape=shape((16, 288, 768), bf16),
        in_specs=[pl.BlockSpec(memory_space=pl.ANY)],
        out_specs=pl.BlockSpec(memory_space=pltpu.VMEM),
        scratch_shapes=[pltpu.SemaphoreType.DMA],
        compiler_params=pltpu.CompilerParams(vmem_limit_bytes=16 << 20),
        cost_estimate=cost_of(0, 14 << 20),
        name="conv_weights",
    )(w_voc)
    out = whole(
        conv_kernel,
        shape((64, 3072), bf16),
        (flags, up_x, snake_alpha, w_conv),
        scratch=[pltpu.VMEM((4, ROWS, 768), bf16)],
        cost=cost_of(2 * 10**9, 8 << 20, 1 << 18),
        smem=1,
        vmem=32,
    )
    return (mel_next, out.reshape(256, 768))


def solution(mesh):
    in_specs = (
        P(("tm", "sub"), None),
        P(),
        P(None, None, "sub"),
        P("sub", None),
        P(None, "sub"),
        P("sub", None),
        P(),
        P("tm", None),
        P(None, "sub", None),
        P(None, "sub", None),
        P(),
        P(None, "sub", None),
        P(None, "sub", None),
    )
    out_specs = (P("tm", None), P(("tm", "sub"), None))
    return jax.shard_map(program, mesh=mesh, in_specs=in_specs, out_specs=out_specs, check_vma=False)
```

```python
import math

import jax
import jax.numpy as jnp
from jax import lax
from jax.experimental import pallas as pl
from jax.experimental.pallas import tpu as pltpu
from jax.sharding import PartitionSpec as P


HEAD_DIM = 64
BLK = 256
MEL_PAD = 128
OFFSETS = 9

epsilon = 1e-06
bf16 = jnp.bfloat16
f32 = jnp.float32


def norm_rows(rows, offset_row, scale_row):
    rows = rows.astype(f32)
    center = jnp.mean(rows, axis=-1, keepdims=True)
    square = jnp.mean(rows * rows, axis=-1, keepdims=True)
    spread = square - center * center
    return (rows - center) * lax.rsqrt(spread + epsilon) * (1.0 + scale_row) + offset_row


def mm(a, b):
    return jnp.dot(a, b, preferred_element_type=f32)


def mm_t(a, b):
    return lax.dot_general(a, b, (((1,), (1,)), ((), ())), preferred_element_type=f32)


def vmem_specs(n):
    return [pl.BlockSpec(memory_space=pltpu.VMEM)] * n


def whole(kernel, out_shapes, args, scratch=(), cost=None, smem=0, vmem=24):
    single = not isinstance(out_shapes, (tuple, list))
    return pl.pallas_call(
        kernel,
        out_shape=out_shapes,
        in_specs=[pl.BlockSpec(memory_space=pltpu.SMEM)] * smem + vmem_specs(len(args) - smem),
        out_specs=vmem_specs(1)[0] if single else vmem_specs(len(out_shapes)),
        scratch_shapes=list(scratch),
        compiler_params=pltpu.CompilerParams(vmem_limit_bytes=vmem << 20),
        cost_estimate=cost,
    )(*args)


def cost_of(flops, nbytes, trans=0):
    return pl.CostEstimate(flops=flops, bytes_accessed=nbytes, transcendentals=trans)


def first_weights_kernel(
    w_ref, o_ref, pre_ref, dil_ref, plain_ref, a_ref, b_ref, voc_ref, pre_scratch, sems
):
    moves = (
        (w_ref.at[0], a_ref.at[pl.ds(0, 64), :]),
        (w_ref.at[1], a_ref.at[pl.ds(64, 64), :]),
        (w_ref.at[2], b_ref.at[pl.ds(0, 64), :]),
        (o_ref, b_ref.at[pl.ds(64, 64), :]),
        (dil_ref, voc_ref.at[pl.ds(96, 144), :]),
        (plain_ref, voc_ref.at[pl.ds(240, 144), :]),
        (pre_ref, pre_scratch),
    )
    copies = [pltpu.make_async_copy(src, dst, sems.at[n]) for n, (src, dst) in enumerate(moves)]
    for copy in copies:
        copy.start()
    voc_ref[0:96, :] = jnp.zeros((96, 768), bf16)
    copies[6].wait()
    for k in range(7):
        voc_ref[0:96, 100 * k : 100 * k + 100] = pre_scratch[k]
    for copy in copies[:6]:
        copy.wait()


def mlp_weights_kernel(up_ref, down_ref, out_ref):
    out_ref[0:1024, :] = up_ref[...]
    for k in range(4):
        out_ref[1024 + 256 * k : 1280 + 256 * k, :] = down_ref[:, 256 * k : 256 * k + 256]


TAP_ORDER = (2, 3, 4, 5, 6, 7, 0, 1)


def upsample_weights_kernel(w_ref, out_ref):
    for s in range(16):
        for t, tap in enumerate(TAP_ORDER):
            out_ref[s, :, 48 * t : 48 * t + 48] = w_ref[tap, :, 48 * s : 48 * s + 48]


def attention_kernel(flag_ref, mod_ref, *refs):
    row_refs, weight_refs = refs[:8], refs[8:16]
    o0, o1, o2, o3, rows, w_a, w_v, w_out, heads, sems = refs[16:]
    copies = []
    for n, ref in enumerate(row_refs):
        copies.append((ref, rows.at[pl.ds(64 * n, 64), :]))
    for h in range(4):
        first_half, second_half = weight_refs[2 * h], weight_refs[2 * h + 1]
        copies.append((first_half, w_a.at[h]))
        copies.append((second_half.at[pl.ds(0, 64), :], w_v.at[h]))
        copies.append((second_half.at[pl.ds(64, 64), :], w_out.at[pl.ds(64 * h, 64), :]))
    copies = [pltpu.make_async_copy(src, dst, sems.at[n]) for n, (src, dst) in enumerate(copies)]
    for copy in copies:
        copy.start()
    first = flag_ref[0] > 0
    scale = 1.0 / math.sqrt(HEAD_DIM)
    for copy in copies[:8]:
        copy.wait()
    normed = norm_rows(rows[...], mod_ref[0:1, :], mod_ref[1:2, :]).astype(bf16)
    own, back = normed[:BLK], normed[BLK:]
    for copy in copies[8:]:
        copy.wait()
    for h in range(4):
        qk = mm_t(own, w_a[h]).astype(bf16)
        q, k = qk[:, 0:64], qk[:, 64:128]
        v = mm_t(own, w_v[h]).astype(bf16)
        kb = mm_t(back, w_a[h, 64:128, :]).astype(bf16)
        vb = mm_t(back, w_v[h]).astype(bf16)
        s_own = mm_t(q, k) * scale
        s_back = mm_t(q, kb) * scale
        s_back = jnp.where(first, -1e30, s_back)
        top = jnp.maximum(
            jnp.max(s_own, axis=-1, keepdims=True), jnp.max(s_back, axis=-1, keepdims=True)
        )
        e_own = jnp.exp(s_own - top)
        e_back = jnp.exp(s_back - top)
        total = jnp.sum(e_own, axis=-1, keepdims=True) + jnp.sum(e_back, axis=-1, keepdims=True)
        inv = 1.0 / total
        p_own = (e_own * inv).astype(bf16)
        p_back = (e_back * inv).astype(bf16)
        heads[:, 64 * h : 64 * h + 64] = (mm(p_own, v) + mm(p_back, vb)).astype(bf16)
    total = mm(heads[...], w_out[...]).astype(bf16)
    for k, out in enumerate((o0, o1, o2, o3)):
        out[...] = total[64 * k : 64 * k + 64]


def sum_of(p0, p1, p2, p3):
    return (p0[...].astype(f32) + p1[...].astype(f32)) + (p2[...].astype(f32) + p3[...].astype(f32))


def after_attention_kernel(p0, p1, p2, p3, frames_ref, mod_ref, mixed_ref, norm_ref):
    attn = sum_of(p0, p1, p2, p3)
    mixed = (frames_ref[...].astype(f32) + mod_ref[2:3, :] * attn).astype(bf16)
    mixed_ref[...] = mixed
    norm_ref[...] = norm_rows(mixed, mod_ref[3:4, :], mod_ref[4:5, :]).astype(bf16)


def mlp_kernel(h0, h1, h2, h3, w0, w1, w2, w3, o0, o1, o2, o3, acc):
    h = jnp.concatenate([h0[...], h1[...], h2[...], h3[...]], axis=0)
    for i, w in enumerate((w0, w1, w2, w3)):
        up = mm(h, w[0:1024, :])
        hid = jax.nn.gelu(up, approximate=True).astype(bf16)
        for k in range(4):
            part = mm(hid, w[1024 + 256 * k : 1280 + 256 * k, :])
            cols = slice(256 * k, 256 * k + 256)
            if i == 0:
                acc[:, cols] = part
            elif i < 3:
                acc[:, cols] += part
            else:
                value = (acc[:, cols] + part).astype(bf16)
                for n, out in enumerate((o0, o1, o2, o3)):
                    out[:, cols] = value[64 * n : 64 * n + 64]


def after_mlp_kernel(p0, p1, p2, p3, mixed_ref, mod_ref, wv_ref, noisy_ref, out_ref):
    feed = sum_of(p0, p1, p2, p3)
    final = (mixed_ref[...].astype(f32) + mod_ref[5:6, :] * feed).astype(bf16)
    normed = norm_rows(final, mod_ref[6:7, :], mod_ref[7:8, :]).astype(bf16)
    mel = noisy_ref[...] + 0.5 * mm(normed, wv_ref[...])
    for s in range(16):
        out_ref[s] = mel


def placed_kernel(comp_ref, full_ref, here_ref):
    earlier = lax.broadcasted_iota(jnp.int32, (100, 192), 1) < 96
    full_ref[...] = jnp.zeros(full_ref.shape, bf16)
    here_ref[...] = jnp.zeros(here_ref.shape, bf16)
    here = [comp_ref[100 * j : 100 * j + 100, 0:192] for j in range(7)]
    near = [comp_ref[100 * j : 100 * j + 100, 192:384] for j in range(7)]
    for d in range(OFFSETS):
        value = jnp.zeros((100, 192), f32)
        if 0 <= d - 1 < 7:
            value = here[d - 1]
            here_ref[MEL_PAD * d : MEL_PAD * d + 100, :] = value.astype(bf16)
        if d < 7:
            value = value + jnp.where(earlier, near[d], 0.0)
        if 0 <= d - 2 < 7:
            value = value + jnp.where(earlier, 0.0, near[d - 2])
        full_ref[MEL_PAD * d : MEL_PAD * d + 100, :] = value.astype(bf16)


EXT = 1056


def upsample_kernel(flag_ref, mel_ref, before_ref, after_ref, full_ref, here_ref, out_ref, ext, up):
    ext[...] = jnp.zeros((EXT, MEL_PAD), f32)
    ext[0:8, 0:100] = before_ref[...]
    for s in range(16):
        ext[8 + 64 * s : 72 + 64 * s, 0:100] = mel_ref[s]
    ext[1032:1040, 0:100] = after_ref[...]
    cols = [ext[3 + k : 3 + k + 1032, :].astype(bf16) for k in range(OFFSETS)]
    up[...] = mm(jnp.concatenate(cols, axis=1), full_ref[...])
    earlier = lax.broadcasted_iota(jnp.int32, (8, 192), 1) < 96
    row = lax.broadcasted_iota(jnp.int32, (8, 192), 0)
    for which, base, r in ((0, 0, 1), (1, 1024, 0)):
        edge_cols = [ext[base + 3 + k : base + 11 + k, :].astype(bf16) for k in range(OFFSETS)]
        edge = mm(jnp.concatenate(edge_cols, axis=1), here_ref[...])
        lanes = earlier if which == 0 else jnp.logical_not(earlier)
        use = (flag_ref[which] > 0) & (row == r) & lanes
        up[base : base + 8, :] = jnp.where(use, edge, up[base : base + 8, :])
    for s in range(16):
        out_ref[s] = up[64 * s : 64 * s + ROWS, :].astype(bf16)


PI_PARTS = (3.140625, 0.000965118408203125, 2.5331974029541016e-06, 1.984187258941006e-09)


def sin_squared(x):
    k = jnp.round(x * (1.0 / math.pi))
    r = x
    for part in PI_PARTS:
        r = r - k * part
    z = r * r
    poly = -2.3889859e-08 * z + 2.7525562e-06
    poly = poly * z - 1.9840874e-04
    poly = poly * z + 8.3333310e-03
    poly = poly * z - 1.6666667e-01
    sine = r + r * (z * poly)
    return sine * sine


def snake_act(values, alpha_row, inverse_row):
    return values + sin_squared(alpha_row * values) * inverse_row


def shifted(plane, by):
    return pltpu.roll(plane, by % plane.shape[0], 0)


ROWS = 72


X_STEPS = (0, 3, 1, 2)


def shard_of(place_ref, which, step):
    return ((place_ref[0] + X_STEPS[step]) & 3) * 4 + (place_ref[1] ^ which)


def merge_kernel(own, left, right, far_top, far_bottom, pre_ref, conv_ref, sems):
    moves = []
    for n, ref in enumerate((own, left, right)):
        moves.append((ref.at[pl.ds(0, 96), :], pre_ref.at[n]))
        moves.append((ref.at[pl.ds(96, 288), :], conv_ref.at[n]))
    moves.append((far_top.at[pl.ds(0, 96), :], pre_ref.at[3]))
    moves.append((far_top.at[pl.ds(96, 96), :], conv_ref.at[3, pl.ds(0, 96), :]))
    moves.append((far_bottom, conv_ref.at[3, pl.ds(96, 192), :]))
    copies = [pltpu.make_async_copy(src, dst, sems.at[n]) for n, (src, dst) in enumerate(moves)]
    for copy in copies:
        copy.start()
    for copy in copies:
        copy.wait()


def prelude_weights_kernel(place_ref, p0, p1, p2, p3, out_ref, sems):
    copies = [
        pltpu.make_async_copy(
            ref.at[step], out_ref.at[shard_of(place_ref, which, step)], sems.at[which, step]
        )
        for which, ref in enumerate((p0, p1, p2, p3))
        for step in range(4)
    ]
    for copy in copies:
        copy.start()
    for copy in copies:
        copy.wait()


def conv_kernel(
    flag_ref, place_ref, up_ref, alpha_ref, c0, c1, c2, c3, out_ref, planes, w_ref, sems
):
    copies = [
        [
            pltpu.make_async_copy(
                ref.at[step, pl.ds(144 * k, 144), :],
                w_ref.at[shard_of(place_ref, which, step), pl.ds(144 * k, 144), :],
                sems.at[k, which, step],
            )
            for which, ref in enumerate((c0, c1, c2, c3))
            for step in range(4)
        ]
        for k in range(2)
    ]
    for half in copies:
        for copy in half:
            copy.start()
    first = flag_ref[0] > 0
    last = flag_ref[1] > 0
    row = lax.broadcasted_iota(jnp.int32, (ROWS, 768), 0)
    outside = (first & (row == 0)) | (last & (row == 65))
    for s in range(16):
        for p in range(4):
            planes[p, :, 48 * s : 48 * s + 48] = up_ref[s, :, 48 * p : 48 * p + 48]
    a1 = alpha_ref[0:1, :]
    a2 = alpha_ref[1:2, :]
    i1 = 1.0 / a1
    i2 = 1.0 / a2

    def weight(base, tap):
        return jnp.concatenate(
            [w_ref[s, base + 48 * tap : base + 48 * tap + 48, :] for s in range(16)], axis=0
        )

    ups = []
    acts = []
    for p in range(4):
        u = jnp.where(outside, 0.0, planes[p].astype(f32))
        ups.append(u)
        acts.append(snake_act(u, a1, i1).astype(bf16))
    act = jnp.concatenate(acts, axis=0)
    for copy in copies[0]:
        copy.wait()
    y = [mm(act, weight(0, tap)) for tap in range(3)]
    y = [[v[ROWS * p : ROWS * p + ROWS] for p in range(4)] for v in y]
    acts = []
    for p in range(4):
        before = y[0][0] if p == 3 else shifted(y[0][p + 1], 1)
        after = y[2][3] if p == 0 else shifted(y[2][p - 1], -1)
        inner = before + y[1][p] + after
        acts.append(jnp.where(outside, 0.0, snake_act(inner, a2, i2)).astype(bf16))
    act = jnp.concatenate(acts, axis=0)
    for copy in copies[1]:
        copy.wait()
    y = [mm(act, weight(144, tap)) for tap in range(3)]
    y = [[v[ROWS * p : ROWS * p + ROWS] for p in range(4)] for v in y]
    for p in range(4):
        before = y[0][p - 1] if p >= 1 else shifted(y[0][3], 1)
        after = y[2][p + 1] if p <= 2 else shifted(y[2][0], -1)
        total = ups[p] + (before + y[1][p] + after)
        out_ref[:, 768 * p : 768 * p + 768] = shifted(total, -1)[0:64].astype(bf16)


def exchange(value, groups=None, axis="sub"):
    return lax.all_to_all(value, axis, 0, 0, tiled=True, axis_index_groups=groups)


def device(y_hi, z, x, y_lo, core):
    return (y_hi * 8 + z) * 16 + x * 4 + y_lo * 2 + core


OTHER_Y = [
    (device(h, z, x, y, c), device(1 - h, z, x, 1 - y, c))
    for h in range(2)
    for z in range(8)
    for x in range(4)
    for y in range(2)
    for c in range(2)
]
OTHER_GROUPS = [
    [device(y ^ side, z, x, y, c) for x in range(4) for y in range(2) for c in range(2)]
    for side in range(2)
    for z in range(8)
]


def program(
    frames,
    modulation,
    w_project,
    w_heads_out,
    w_up,
    w_down,
    w_velocity,
    noisy_mel,
    w_prelude,
    w_upsample,
    snake_alpha,
    w_dilated,
    w_plain,
):
    own_rows = frames.shape[0]
    sub_index = lax.axis_index("sub")
    time_index = lax.axis_index("tm")
    n_sub = lax.axis_size("sub")
    n_tm = lax.axis_size("tm")
    n_all = n_sub * n_tm
    both = ("tm", "sub")
    shape = jax.ShapeDtypeStruct
    here_index = time_index * n_sub + sub_index

    to_right = [(i, (i + 4) % 16) for i in range(16)]
    to_left = [(i, (i - 4) % 16) for i in range(16)]
    own_a, own_b, w_voc = pl.pallas_call(
        first_weights_kernel,
        out_shape=(shape((128, 1024), bf16), shape((128, 1024), bf16), shape((384, 768), bf16)),
        in_specs=[pl.BlockSpec(memory_space=pl.ANY)] * 5,
        out_specs=vmem_specs(3),
        scratch_shapes=[pltpu.VMEM((7, 96, 100), bf16), pltpu.SemaphoreType.DMA((7,))],
        compiler_params=pltpu.CompilerParams(vmem_limit_bytes=60 << 20),
        cost_estimate=cost_of(0, 3 << 20),
        name="first_weights",
    )(
        jnp.swapaxes(w_project, 1, 2),
        w_heads_out,
        w_prelude,
        w_dilated.reshape(144, 768),
        w_plain.reshape(144, 768),
    )
    back_frames = lax.ppermute(frames, both, [(i, i + 4) for i in range(n_all - 4)])
    left_a = lax.ppermute(own_a, "sub", to_right)
    right_b = lax.ppermute(own_b, "sub", to_left)
    left_b = lax.ppermute(own_b, "sub", to_right)
    right_a = lax.ppermute(own_a, "sub", to_left)
    far_a = lax.ppermute(left_a, "sub", to_right)
    far_b = lax.ppermute(right_b, "sub", to_left)

    voc_left = lax.ppermute(w_voc, "sub", to_right)
    voc_right = lax.ppermute(w_voc, "sub", to_left)
    voc_top = lax.ppermute(voc_left[:192], "sub", to_right)
    voc_bottom = lax.ppermute(voc_right[192:], "sub", to_left)
    pre_shape, conv_shape = shape((4, 96, 768), bf16), shape((4, 288, 768), bf16)
    raw = pl.BlockSpec(memory_space=pl.ANY)
    pre_own, conv_own = pl.pallas_call(
        merge_kernel,
        out_shape=(pre_shape, conv_shape),
        in_specs=[raw] * 5,
        out_specs=vmem_specs(2),
        scratch_shapes=[pltpu.SemaphoreType.DMA((9,))],
        compiler_params=pltpu.CompilerParams(vmem_limit_bytes=60 << 20),
        cost_estimate=cost_of(0, 5 << 20),
        name="voc_merge",
    )(w_voc, voc_left, voc_right, voc_top, voc_bottom)
    swap = [(i, i ^ 1) for i in range(16)]
    pre_y = lax.ppermute(pre_own, both, OTHER_Y)
    conv_y = lax.ppermute(conv_own, both, OTHER_Y)
    pre_core = lax.ppermute(pre_own, "sub", swap)
    conv_core = lax.ppermute(conv_own, "sub", swap)
    pre_both = lax.ppermute(pre_y, "sub", swap)
    conv_both = lax.ppermute(conv_y, "sub", swap)
    place = jnp.stack([sub_index // 4, lax.rem(sub_index, 4)]).astype(jnp.int32)

    beside = [[(i, i ^ k) for i in range(16)] for k in (1, 2, 3)]
    block = [frames] + [lax.ppermute(frames, "sub", beside[k - 1]) for k in (1, 2, 3)]
    back = [back_frames] + [lax.ppermute(back_frames, "sub", beside[k - 1]) for k in (1, 2, 3)]

    own_mlp = whole(
        mlp_weights_kernel, shape((2048, 256), bf16), (w_up, w_down), cost=cost_of(0, 2 << 20)
    )
    other_core = lax.ppermute(own_mlp, "sub", [(i, i ^ 1) for i in range(16)])
    other_y = lax.ppermute(own_mlp, both, OTHER_Y)
    other_both = lax.ppermute(other_y, "sub", [(i, i ^ 1) for i in range(16)])

    ups = whole(
        upsample_weights_kernel, shape((16, 96, 384), bf16), (w_upsample,), cost=cost_of(0, 3 << 20)
    )

    is_first = (time_index == 0) & (sub_index < 4)
    quarter = shape((own_rows, 1024), bf16)
    partial = pl.pallas_call(
        attention_kernel,
        out_shape=(quarter,) * 4,
        in_specs=[pl.BlockSpec(memory_space=pltpu.SMEM)]
        + vmem_specs(1)
        + [pl.BlockSpec(memory_space=pl.ANY)] * 16,
        out_specs=vmem_specs(4),
        scratch_shapes=[
            pltpu.VMEM((2 * BLK, 1024), bf16),
            pltpu.VMEM((4, 128, 1024), bf16),
            pltpu.VMEM((4, 64, 1024), bf16),
            pltpu.VMEM((256, 1024), bf16),
            pltpu.VMEM((BLK, 256), bf16),
            pltpu.SemaphoreType.DMA((20,)),
        ],
        compiler_params=pltpu.CompilerParams(vmem_limit_bytes=60 << 20),
        cost_estimate=cost_of(10**9, 4 << 20, 1 << 19),
        name="attention",
    )(
        is_first.astype(jnp.int32).reshape(1),
        modulation,
        *block,
        *back,
        own_a,
        own_b,
        left_a,
        left_b,
        right_a,
        right_b,
        far_a,
        far_b,
    )
    ups = exchange(ups, OTHER_GROUPS, both)
    parts = [partial[0]] + [lax.ppermute(partial[k], "sub", beside[k - 1]) for k in (1, 2, 3)]
    mixed_rows, own_norm = whole(
        after_attention_kernel,
        (quarter, quarter),
        (*parts, frames, modulation),
        cost=cost_of(10**6, 1 << 20),
    )

    own_norm, ups = lax.optimization_barrier((own_norm, ups))
    across = [(i, (i + 8) % 16) for i in range(16)]
    second = [
        own_norm,
        lax.ppermute(own_norm, "sub", across),
        lax.ppermute(own_norm, "sub", to_right),
        lax.ppermute(own_norm, "sub", to_left),
    ]
    partial = whole(
        mlp_kernel,
        (quarter,) * 4,
        (*second, own_mlp, other_core, other_y, other_both),
        scratch=[pltpu.VMEM((256, 1024), f32)],
        cost=cost_of(11 * 10**8, 5 << 20, 1 << 18),
    )
    parts = [
        partial[0],
        lax.ppermute(partial[1], "sub", across),
        lax.ppermute(partial[2], "sub", to_left),
        lax.ppermute(partial[3], "sub", to_right),
    ]
    noisy_own = lax.dynamic_slice_in_dim(noisy_mel, sub_index * own_rows, own_rows, 0)
    copies = whole(
        after_mlp_kernel,
        shape((16, own_rows, 100), f32),
        (*parts, mixed_rows, modulation, w_velocity, noisy_own),
        cost=cost_of(10**7, 1 << 20),
    )
    mel_all = exchange(copies)
    mel_next = mel_all.reshape(-1, 100)

    pre_all = pl.pallas_call(
        prelude_weights_kernel,
        out_shape=shape((16, 96, 768), bf16),
        in_specs=[pl.BlockSpec(memory_space=pltpu.SMEM)] + [raw] * 4,
        out_specs=pl.BlockSpec(memory_space=pltpu.VMEM),
        scratch_shapes=[pltpu.SemaphoreType.DMA((4, 4))],
        compiler_params=pltpu.CompilerParams(vmem_limit_bytes=60 << 20),
        cost_estimate=cost_of(0, 5 << 20),
        name="prelude_weights",
    )(place, pre_own, pre_core, pre_y, pre_both).reshape(1536, 768)
    comp = lax.dot_general(
        pre_all, ups.reshape(1536, 384), (((0,), (0,)), ((), ())), preferred_element_type=f32
    )
    w_full, w_here = whole(
        placed_kernel,
        (shape((OFFSETS * MEL_PAD, 192), bf16), shape((OFFSETS * MEL_PAD, 192), bf16)),
        (comp,),
        cost=cost_of(10**6, 2 << 20),
    )

    before = lax.ppermute(mel_all[15, 56:], "tm", [(i, i + 1) for i in range(n_tm - 1)])
    after = lax.ppermute(mel_all[0, :8], "tm", [(i + 1, i) for i in range(n_tm - 1)])
    windows = whole(
        upsample_kernel,
        shape((16, ROWS, 192), bf16),
        (
            jnp.stack([time_index == 0, time_index == n_tm - 1]).astype(jnp.int32),
            mel_all,
            before,
            after,
            w_full,
            w_here,
        ),
        scratch=[pltpu.VMEM((EXT, MEL_PAD), f32), pltpu.VMEM((1032, 192), f32)],
        cost=cost_of(5 * 10**8, 2 << 20),
        smem=1,
    )
    up_x = exchange(windows)

    flags = jnp.stack([here_index == 0, here_index == n_all - 1]).astype(jnp.int32)
    out = pl.pallas_call(
        conv_kernel,
        out_shape=shape((64, 3072), bf16),
        in_specs=[pl.BlockSpec(memory_space=pltpu.SMEM)] * 2 + vmem_specs(2) + [raw] * 4,
        out_specs=pl.BlockSpec(memory_space=pltpu.VMEM),
        scratch_shapes=[
            pltpu.VMEM((4, ROWS, 768), bf16),
            pltpu.VMEM((16, 288, 768), bf16),
            pltpu.SemaphoreType.DMA((2, 4, 4)),
        ],
        compiler_params=pltpu.CompilerParams(vmem_limit_bytes=60 << 20),
        cost_estimate=cost_of(2 * 10**9, 8 << 20, 1 << 18),
        name="convolutions",
    )(flags, place, up_x, snake_alpha, conv_own, conv_core, conv_y, conv_both)
    return (mel_next, out.reshape(256, 768))


def solution(mesh):
    in_specs = (
        P(("tm", "sub"), None),
        P(),
        P(None, None, "sub"),
        P("sub", None),
        P(None, "sub"),
        P("sub", None),
        P(),
        P("tm", None),
        P(None, "sub", None),
        P(None, "sub", None),
        P(),
        P(None, "sub", None),
        P(None, "sub", None),
    )
    out_specs = (P("tm", None), P(("tm", "sub"), None))
    return jax.shard_map(program, mesh=mesh, in_specs=in_specs, out_specs=out_specs, check_vma=False)
```

```python
import math

import jax
import jax.numpy as jnp
from jax import lax
from jax.experimental import pallas as pl
from jax.experimental.pallas import tpu as pltpu
from jax.sharding import PartitionSpec as P


HEAD_DIM = 64
BLK = 256
MEL_PAD = 128
OFFSETS = 9

epsilon = 1e-06
bf16 = jnp.bfloat16
f32 = jnp.float32


def norm_rows(rows, offset_row, scale_row):
    rows = rows.astype(f32)
    center = jnp.mean(rows, axis=-1, keepdims=True)
    square = jnp.mean(rows * rows, axis=-1, keepdims=True)
    spread = square - center * center
    return (rows - center) * lax.rsqrt(spread + epsilon) * (1.0 + scale_row) + offset_row


def mm(a, b):
    return jnp.dot(a, b, preferred_element_type=f32)


def mm_t(a, b):
    return lax.dot_general(a, b, (((1,), (1,)), ((), ())), preferred_element_type=f32)


def vmem_specs(n):
    return [pl.BlockSpec(memory_space=pltpu.VMEM)] * n


def whole(kernel, out_shapes, args, scratch=(), cost=None, smem=0, vmem=24):
    single = not isinstance(out_shapes, (tuple, list))
    return pl.pallas_call(
        kernel,
        out_shape=out_shapes,
        in_specs=[pl.BlockSpec(memory_space=pltpu.SMEM)] * smem + vmem_specs(len(args) - smem),
        out_specs=vmem_specs(1)[0] if single else vmem_specs(len(out_shapes)),
        scratch_shapes=list(scratch),
        compiler_params=pltpu.CompilerParams(vmem_limit_bytes=vmem << 20),
        cost_estimate=cost,
    )(*args)


def cost_of(flops, nbytes, trans=0):
    return pl.CostEstimate(flops=flops, bytes_accessed=nbytes, transcendentals=trans)


def first_weights_kernel(
    w_ref, o_ref, pre_ref, dil_ref, plain_ref, a_ref, b_ref, voc_ref, pre_scratch, sems
):
    moves = (
        (w_ref.at[0], a_ref.at[pl.ds(0, 64), :]),
        (w_ref.at[1], a_ref.at[pl.ds(64, 64), :]),
        (w_ref.at[2], b_ref.at[pl.ds(0, 64), :]),
        (o_ref, b_ref.at[pl.ds(64, 64), :]),
        (dil_ref, voc_ref.at[pl.ds(96, 144), :]),
        (plain_ref, voc_ref.at[pl.ds(240, 144), :]),
        (pre_ref, pre_scratch),
    )
    copies = [pltpu.make_async_copy(src, dst, sems.at[n]) for n, (src, dst) in enumerate(moves)]
    for copy in copies:
        copy.start()
    voc_ref[0:96, :] = jnp.zeros((96, 768), bf16)
    copies[6].wait()
    for k in range(7):
        voc_ref[0:96, 100 * k : 100 * k + 100] = pre_scratch[k]
    for copy in copies[:6]:
        copy.wait()


def mlp_weights_kernel(up_ref, down_ref, out_ref):
    out_ref[0:1024, :] = up_ref[...]
    for k in range(4):
        out_ref[1024 + 256 * k : 1280 + 256 * k, :] = down_ref[:, 256 * k : 256 * k + 256]


TAP_ORDER = (2, 3, 4, 5, 6, 7, 0, 1)


def upsample_weights_kernel(w_ref, out_ref):
    def half(g, carry):
        lanes = pl.ds(pl.multiple_of(384 * g, 384), 384)
        for t, tap in enumerate(TAP_ORDER):
            rows = w_ref[tap, :, lanes]
            for i in range(8):
                out_ref[8 * g + i, :, 48 * t : 48 * t + 48] = rows[:, 48 * i : 48 * i + 48]
        return carry

    lax.fori_loop(0, 2, half, 0)


def attention_kernel(flag_ref, mod_ref, *refs):
    row_refs, weight_refs = refs[:8], refs[8:16]
    o0, o1, o2, o3, rows, w_a, w_v, w_out, heads, sems = refs[16:]
    copies = []
    for n, ref in enumerate(row_refs):
        copies.append((ref, rows.at[pl.ds(64 * n, 64), :]))
    for h in range(4):
        first_half, second_half = weight_refs[2 * h], weight_refs[2 * h + 1]
        copies.append((first_half, w_a.at[h]))
        copies.append((second_half.at[pl.ds(0, 64), :], w_v.at[h]))
        copies.append((second_half.at[pl.ds(64, 64), :], w_out.at[pl.ds(64 * h, 64), :]))
    copies = [pltpu.make_async_copy(src, dst, sems.at[n]) for n, (src, dst) in enumerate(copies)]
    for copy in copies:
        copy.start()
    first = flag_ref[0] > 0
    scale = 1.0 / math.sqrt(HEAD_DIM)
    for copy in copies[:8]:
        copy.wait()
    normed = norm_rows(rows[...], mod_ref[0:1, :], mod_ref[1:2, :]).astype(bf16)
    own, back = normed[:BLK], normed[BLK:]
    for copy in copies[8:]:
        copy.wait()

    def one_head(h):
        qk = mm_t(own, w_a[h]).astype(bf16)
        q, k = qk[:, 0:64], qk[:, 64:128]
        v = mm_t(own, w_v[h]).astype(bf16)
        kb = mm_t(back, w_a[h, 64:128, :]).astype(bf16)
        vb = mm_t(back, w_v[h]).astype(bf16)
        s_own = mm_t(q, k) * scale
        s_back = mm_t(q, kb) * scale
        s_back = jnp.where(first, -1e30, s_back)
        top = jnp.maximum(
            jnp.max(s_own, axis=-1, keepdims=True), jnp.max(s_back, axis=-1, keepdims=True)
        )
        e_own = jnp.exp(s_own - top)
        e_back = jnp.exp(s_back - top)
        total = jnp.sum(e_own, axis=-1, keepdims=True) + jnp.sum(e_back, axis=-1, keepdims=True)
        inv = 1.0 / total
        p_own = (e_own * inv).astype(bf16)
        p_back = (e_back * inv).astype(bf16)
        heads[h] = (mm(p_own, v) + mm(p_back, vb)).astype(bf16)

    lax.fori_loop(0, 4, lambda h, c: (one_head(h), c)[1], 0)
    outs = jnp.concatenate([heads[h] for h in range(4)], axis=1)
    total = mm(outs, w_out[...]).astype(bf16)
    for k, out in enumerate((o0, o1, o2, o3)):
        out[...] = total[64 * k : 64 * k + 64]


def sum_of(p0, p1, p2, p3):
    return (p0[...].astype(f32) + p1[...].astype(f32)) + (p2[...].astype(f32) + p3[...].astype(f32))


def after_attention_kernel(p0, p1, p2, p3, frames_ref, mod_ref, mixed_ref, norm_ref):
    attn = sum_of(p0, p1, p2, p3)
    mixed = (frames_ref[...].astype(f32) + mod_ref[2:3, :] * attn).astype(bf16)
    mixed_ref[...] = mixed
    norm_ref[...] = norm_rows(mixed, mod_ref[3:4, :], mod_ref[4:5, :]).astype(bf16)


def mlp_kernel(h0, h1, h2, h3, w0, w1, w2, w3, o0, o1, o2, o3, acc):
    h = jnp.concatenate([h0[...], h1[...], h2[...], h3[...]], axis=0)
    for i, w in enumerate((w0, w1, w2, w3)):
        up = mm(h, w[0:1024, :])
        hid = jax.nn.gelu(up, approximate=True).astype(bf16)
        for k in range(4):
            part = mm(hid, w[1024 + 256 * k : 1280 + 256 * k, :])
            cols = slice(256 * k, 256 * k + 256)
            if i == 0:
                acc[:, cols] = part
            elif i < 3:
                acc[:, cols] += part
            else:
                value = (acc[:, cols] + part).astype(bf16)
                for n, out in enumerate((o0, o1, o2, o3)):
                    out[:, cols] = value[64 * n : 64 * n + 64]


def after_mlp_kernel(p0, p1, p2, p3, mixed_ref, mod_ref, wv_ref, noisy_ref, out_ref):
    feed = sum_of(p0, p1, p2, p3)
    final = (mixed_ref[...].astype(f32) + mod_ref[5:6, :] * feed).astype(bf16)
    normed = norm_rows(final, mod_ref[6:7, :], mod_ref[7:8, :]).astype(bf16)
    mel = noisy_ref[...] + 0.5 * mm(normed, wv_ref[...])
    for s in range(16):
        out_ref[s] = mel


def placed_kernel(comp_ref, full_ref, here_ref):
    earlier = lax.broadcasted_iota(jnp.int32, (100, 192), 1) < 96
    full_ref[...] = jnp.zeros(full_ref.shape, bf16)
    here_ref[...] = jnp.zeros(here_ref.shape, bf16)
    here = [comp_ref[100 * j : 100 * j + 100, 0:192] for j in range(7)]
    near = [comp_ref[100 * j : 100 * j + 100, 192:384] for j in range(7)]
    for d in range(OFFSETS):
        value = jnp.zeros((100, 192), f32)
        if 0 <= d - 1 < 7:
            value = here[d - 1]
            here_ref[MEL_PAD * d : MEL_PAD * d + 100, :] = value.astype(bf16)
        if d < 7:
            value = value + jnp.where(earlier, near[d], 0.0)
        if 0 <= d - 2 < 7:
            value = value + jnp.where(earlier, 0.0, near[d - 2])
        full_ref[MEL_PAD * d : MEL_PAD * d + 100, :] = value.astype(bf16)


EXT = 1056


def upsample_kernel(flag_ref, mel_ref, before_ref, after_ref, full_ref, here_ref, out_ref, ext, up):
    ext[...] = jnp.zeros((EXT, MEL_PAD), f32)
    ext[0:8, 0:100] = before_ref[...]
    for s in range(16):
        ext[8 + 64 * s : 72 + 64 * s, 0:100] = mel_ref[s]
    ext[1032:1040, 0:100] = after_ref[...]
    cols = [ext[3 + k : 3 + k + 1032, :].astype(bf16) for k in range(OFFSETS)]
    up[...] = mm(jnp.concatenate(cols, axis=1), full_ref[...])
    earlier = lax.broadcasted_iota(jnp.int32, (8, 192), 1) < 96
    row = lax.broadcasted_iota(jnp.int32, (8, 192), 0)
    for which, base, r in ((0, 0, 1), (1, 1024, 0)):
        edge_cols = [ext[base + 3 + k : base + 11 + k, :].astype(bf16) for k in range(OFFSETS)]
        edge = mm(jnp.concatenate(edge_cols, axis=1), here_ref[...])
        lanes = earlier if which == 0 else jnp.logical_not(earlier)
        use = (flag_ref[which] > 0) & (row == r) & lanes
        up[base : base + 8, :] = jnp.where(use, edge, up[base : base + 8, :])
    for s in range(16):
        out_ref[s] = up[64 * s : 64 * s + ROWS, :].astype(bf16)


PI_PARTS = (3.140625, 0.000965118408203125, 2.5331974029541016e-06, 1.984187258941006e-09)


def sin_squared(x):
    k = jnp.round(x * (1.0 / math.pi))
    r = x
    for part in PI_PARTS:
        r = r - k * part
    z = r * r
    poly = -2.3889859e-08 * z + 2.7525562e-06
    poly = poly * z - 1.9840874e-04
    poly = poly * z + 8.3333310e-03
    poly = poly * z - 1.6666667e-01
    sine = r + r * (z * poly)
    return sine * sine


def snake_act(values, alpha_row, inverse_row):
    return values + sin_squared(alpha_row * values) * inverse_row


def shifted(plane, by):
    return pltpu.roll(plane, by % plane.shape[0], 0)


ROWS = 72


X_STEPS = (0, 3, 1, 2)


def shard_of(place_ref, which, step):
    return ((place_ref[0] + X_STEPS[step]) & 3) * 4 + (place_ref[1] ^ which)


def merge_kernel(own, left, right, far_top, far_bottom, pre_ref, dil_ref, plain_ref, sems):
    moves = []
    for n, ref in enumerate((own, left, right)):
        moves.append((ref.at[pl.ds(0, 96), :], pre_ref.at[n]))
        moves.append((ref.at[pl.ds(96, 144), :], dil_ref.at[n]))
        moves.append((ref.at[pl.ds(240, 144), :], plain_ref.at[n]))
    moves.append((far_top.at[pl.ds(0, 96), :], pre_ref.at[3]))
    moves.append((far_top.at[pl.ds(96, 144), :], dil_ref.at[3]))
    moves.append((far_bottom, plain_ref.at[3]))
    copies = [pltpu.make_async_copy(src, dst, sems.at[n]) for n, (src, dst) in enumerate(moves)]
    for copy in copies:
        copy.start()
    for copy in copies:
        copy.wait()


def prelude_weights_kernel(place_ref, p0, p1, p2, p3, out_ref, sems):
    copies = [
        pltpu.make_async_copy(
            ref.at[step], out_ref.at[shard_of(place_ref, which, step)], sems.at[which, step]
        )
        for which, ref in enumerate((p0, p1, p2, p3))
        for step in range(4)
    ]
    for copy in copies:
        copy.start()
    for copy in copies:
        copy.wait()


STRIDE = 80


def conv_kernel(flag_ref, place_ref, up_ref, alpha_ref, *refs):
    out_ref, planes, act_one, act_two, w_one, w_two, sems = refs[8:]
    copies = [
        [
            pltpu.make_async_copy(
                refs[4 * k + which].at[step],
                buf.at[shard_of(place_ref, which, step)],
                sems.at[k, which, step],
            )
            for which in range(4)
            for step in range(4)
        ]
        for k, buf in enumerate((w_one, w_two))
    ]
    for half in copies:
        for copy in half:
            copy.start()
    first = flag_ref[0] > 0
    last = flag_ref[1] > 0
    row = lax.broadcasted_iota(jnp.int32, (ROWS, 256), 0)
    outside = (first & (row == 0)) | (last & (row == 65))

    def gather_channels(g, carry):
        lanes = pl.ds(pl.multiple_of(384 * g, 384), 384)
        for p in range(4):
            parts = [up_ref[8 * g + i, :, 48 * p : 48 * p + 48] for i in range(8)]
            planes[p, :, lanes] = jnp.concatenate(parts, axis=1)
        return carry

    lax.fori_loop(0, 2, gather_channels, 0)
    act_one[...] = jnp.zeros(act_one.shape, bf16)
    act_two[...] = jnp.zeros(act_two.shape, bf16)

    def columns(n):
        return pl.ds(pl.multiple_of(256 * n, 256), 256)

    def up_plane(p, cols):
        return jnp.where(outside, 0.0, planes[p, :, cols].astype(f32))

    def products(act_ref, w_ref, cols):
        act = act_ref[...]
        y = []
        for tap in range(3):
            weight = jnp.concatenate(
                [w_ref[s, 48 * tap : 48 * tap + 48, cols] for s in range(16)], axis=0
            )
            v = mm(act, weight)
            y.append([v[STRIDE * p : STRIDE * p + ROWS] for p in range(4)])
        return y

    def first_act(n, carry):
        cols = columns(n)
        alpha = alpha_ref[0:1, cols]
        for p in range(4):
            value = snake_act(up_plane(p, cols), alpha, 1.0 / alpha).astype(bf16)
            act_one[STRIDE * p : STRIDE * p + ROWS, cols] = value
        return carry

    def first_conv(n, carry):
        cols = columns(n)
        alpha = alpha_ref[1:2, cols]
        y = products(act_one, w_one, cols)
        for p in range(4):
            before = y[0][0] if p == 3 else shifted(y[0][p + 1], 1)
            after = y[2][3] if p == 0 else shifted(y[2][p - 1], -1)
            value = snake_act(before + y[1][p] + after, alpha, 1.0 / alpha)
            value = jnp.where(outside, 0.0, value).astype(bf16)
            act_two[STRIDE * p : STRIDE * p + ROWS, cols] = value
        return carry

    def second_conv(n, carry):
        cols = columns(n)
        y = products(act_two, w_two, cols)
        for p in range(4):
            before = y[0][p - 1] if p >= 1 else shifted(y[0][3], 1)
            after = y[2][p + 1] if p <= 2 else shifted(y[2][0], -1)
            total = up_plane(p, cols) + (before + y[1][p] + after)
            to = pl.ds(pl.multiple_of(768 * p + 256 * n, 256), 256)
            out_ref[:, to] = shifted(total, -1)[0:64].astype(bf16)
        return carry

    lax.fori_loop(0, 3, first_act, 0)
    for copy in copies[0]:
        copy.wait()
    lax.fori_loop(0, 3, first_conv, 0)
    for copy in copies[1]:
        copy.wait()
    lax.fori_loop(0, 3, second_conv, 0)


def exchange(value, groups=None, axis="sub"):
    return lax.all_to_all(value, axis, 0, 0, tiled=True, axis_index_groups=groups)


def device(y_hi, z, x, y_lo, core):
    return (y_hi * 8 + z) * 16 + x * 4 + y_lo * 2 + core


OTHER_Y = [
    (device(h, z, x, y, c), device(1 - h, z, x, 1 - y, c))
    for h in range(2)
    for z in range(8)
    for x in range(4)
    for y in range(2)
    for c in range(2)
]
OTHER_GROUPS = [
    [device(y ^ side, z, x, y, c) for x in range(4) for y in range(2) for c in range(2)]
    for side in range(2)
    for z in range(8)
]


def program(
    frames,
    modulation,
    w_project,
    w_heads_out,
    w_up,
    w_down,
    w_velocity,
    noisy_mel,
    w_prelude,
    w_upsample,
    snake_alpha,
    w_dilated,
    w_plain,
):
    own_rows = frames.shape[0]
    sub_index = lax.axis_index("sub")
    time_index = lax.axis_index("tm")
    n_sub = lax.axis_size("sub")
    n_tm = lax.axis_size("tm")
    n_all = n_sub * n_tm
    both = ("tm", "sub")
    shape = jax.ShapeDtypeStruct
    here_index = time_index * n_sub + sub_index

    to_right = [(i, (i + 4) % 16) for i in range(16)]
    to_left = [(i, (i - 4) % 16) for i in range(16)]
    own_a, own_b, w_voc = pl.pallas_call(
        first_weights_kernel,
        out_shape=(shape((128, 1024), bf16), shape((128, 1024), bf16), shape((384, 768), bf16)),
        in_specs=[pl.BlockSpec(memory_space=pl.ANY)] * 5,
        out_specs=vmem_specs(3),
        scratch_shapes=[pltpu.VMEM((7, 96, 100), bf16), pltpu.SemaphoreType.DMA((7,))],
        compiler_params=pltpu.CompilerParams(vmem_limit_bytes=60 << 20),
        cost_estimate=cost_of(0, 3 << 20),
        name="first_weights",
    )(
        jnp.swapaxes(w_project, 1, 2),
        w_heads_out,
        w_prelude,
        w_dilated.reshape(144, 768),
        w_plain.reshape(144, 768),
    )
    back_frames = lax.ppermute(frames, both, [(i, i + 4) for i in range(n_all - 4)])
    left_a = lax.ppermute(own_a, "sub", to_right)
    right_b = lax.ppermute(own_b, "sub", to_left)
    left_b = lax.ppermute(own_b, "sub", to_right)
    right_a = lax.ppermute(own_a, "sub", to_left)
    far_a = lax.ppermute(left_a, "sub", to_right)
    far_b = lax.ppermute(right_b, "sub", to_left)

    voc_left = lax.ppermute(w_voc, "sub", to_right)
    voc_right = lax.ppermute(w_voc, "sub", to_left)
    voc_top = lax.ppermute(voc_left[:240], "sub", to_right)
    voc_bottom = lax.ppermute(voc_right[240:], "sub", to_left)
    pre_shape, conv_shape = shape((4, 96, 768), bf16), shape((4, 144, 768), bf16)
    raw = pl.BlockSpec(memory_space=pl.ANY)
    pre_own, dil_own, plain_own = pl.pallas_call(
        merge_kernel,
        out_shape=(pre_shape, conv_shape, conv_shape),
        in_specs=[raw] * 5,
        out_specs=vmem_specs(3),
        scratch_shapes=[pltpu.SemaphoreType.DMA((12,))],
        compiler_params=pltpu.CompilerParams(vmem_limit_bytes=60 << 20),
        cost_estimate=cost_of(0, 5 << 20),
        name="voc_merge",
    )(w_voc, voc_left, voc_right, voc_top, voc_bottom)
    beside = [[(i, i ^ k) for i in range(16)] for k in (1, 2, 3)]
    pre_y = lax.ppermute(pre_own, both, OTHER_Y)
    dil_y = lax.ppermute(dil_own, both, OTHER_Y)
    plain_y = lax.ppermute(plain_own, "sub", beside[1])
    pre_core = lax.ppermute(pre_own, "sub", beside[0])
    dil_core = lax.ppermute(dil_own, "sub", beside[0])
    plain_core = lax.ppermute(plain_own, "sub", beside[0])
    pre_both = lax.ppermute(pre_y, "sub", beside[0])
    dil_both = lax.ppermute(dil_y, "sub", beside[0])
    plain_both = lax.ppermute(plain_y, "sub", beside[0])
    place = jnp.stack([sub_index // 4, lax.rem(sub_index, 4)]).astype(jnp.int32)

    block = [frames] + [lax.ppermute(frames, "sub", beside[k - 1]) for k in (1, 2, 3)]
    back = [back_frames] + [lax.ppermute(back_frames, "sub", beside[k - 1]) for k in (1, 2, 3)]

    own_mlp = whole(
        mlp_weights_kernel, shape((2048, 256), bf16), (w_up, w_down), cost=cost_of(0, 2 << 20)
    )
    other_core = lax.ppermute(own_mlp, "sub", [(i, i ^ 1) for i in range(16)])
    other_y = lax.ppermute(own_mlp, both, OTHER_Y)
    other_both = lax.ppermute(other_y, "sub", [(i, i ^ 1) for i in range(16)])

    ups = whole(
        upsample_weights_kernel, shape((16, 96, 384), bf16), (w_upsample,), cost=cost_of(0, 3 << 20)
    )

    is_first = (time_index == 0) & (sub_index < 4)
    quarter = shape((own_rows, 1024), bf16)
    partial = pl.pallas_call(
        attention_kernel,
        out_shape=(quarter,) * 4,
        in_specs=[pl.BlockSpec(memory_space=pltpu.SMEM)]
        + vmem_specs(1)
        + [pl.BlockSpec(memory_space=pl.ANY)] * 16,
        out_specs=vmem_specs(4),
        scratch_shapes=[
            pltpu.VMEM((2 * BLK, 1024), bf16),
            pltpu.VMEM((4, 128, 1024), bf16),
            pltpu.VMEM((4, 64, 1024), bf16),
            pltpu.VMEM((256, 1024), bf16),
            pltpu.VMEM((4, BLK, 64), bf16),
            pltpu.SemaphoreType.DMA((20,)),
        ],
        compiler_params=pltpu.CompilerParams(vmem_limit_bytes=60 << 20),
        cost_estimate=cost_of(10**9, 4 << 20, 1 << 19),
        name="attention",
    )(
        is_first.astype(jnp.int32).reshape(1),
        modulation,
        *block,
        *back,
        own_a,
        own_b,
        left_a,
        left_b,
        right_a,
        right_b,
        far_a,
        far_b,
    )
    ups = exchange(ups, OTHER_GROUPS, both)
    parts = [partial[0]] + [lax.ppermute(partial[k], "sub", beside[k - 1]) for k in (1, 2, 3)]
    mixed_rows, own_norm = whole(
        after_attention_kernel,
        (quarter, quarter),
        (*parts, frames, modulation),
        cost=cost_of(10**6, 1 << 20),
    )

    own_norm, ups = lax.optimization_barrier((own_norm, ups))
    across = [(i, (i + 8) % 16) for i in range(16)]
    second = [
        own_norm,
        lax.ppermute(own_norm, "sub", across),
        lax.ppermute(own_norm, "sub", to_right),
        lax.ppermute(own_norm, "sub", to_left),
    ]
    partial = whole(
        mlp_kernel,
        (quarter,) * 4,
        (*second, own_mlp, other_core, other_y, other_both),
        scratch=[pltpu.VMEM((256, 1024), f32)],
        cost=cost_of(11 * 10**8, 5 << 20, 1 << 18),
    )
    parts = [
        partial[0],
        lax.ppermute(partial[1], "sub", across),
        lax.ppermute(partial[2], "sub", to_left),
        lax.ppermute(partial[3], "sub", to_right),
    ]
    noisy_own = lax.dynamic_slice_in_dim(noisy_mel, sub_index * own_rows, own_rows, 0)
    copies = whole(
        after_mlp_kernel,
        shape((16, own_rows, 100), f32),
        (*parts, mixed_rows, modulation, w_velocity, noisy_own),
        cost=cost_of(10**7, 1 << 20),
    )
    mel_all = exchange(copies)
    mel_next = mel_all.reshape(-1, 100)

    pre_all = pl.pallas_call(
        prelude_weights_kernel,
        out_shape=shape((16, 96, 768), bf16),
        in_specs=[pl.BlockSpec(memory_space=pltpu.SMEM)] + [raw] * 4,
        out_specs=pl.BlockSpec(memory_space=pltpu.VMEM),
        scratch_shapes=[pltpu.SemaphoreType.DMA((4, 4))],
        compiler_params=pltpu.CompilerParams(vmem_limit_bytes=60 << 20),
        cost_estimate=cost_of(0, 5 << 20),
        name="prelude_weights",
    )(place, pre_own, pre_core, pre_y, pre_both).reshape(1536, 768)
    comp = lax.dot_general(
        pre_all, ups.reshape(1536, 384), (((0,), (0,)), ((), ())), preferred_element_type=f32
    )
    w_full, w_here = whole(
        placed_kernel,
        (shape((OFFSETS * MEL_PAD, 192), bf16), shape((OFFSETS * MEL_PAD, 192), bf16)),
        (comp,),
        cost=cost_of(10**6, 2 << 20),
    )

    before = lax.ppermute(mel_all[15, 56:], "tm", [(i, i + 1) for i in range(n_tm - 1)])
    after = lax.ppermute(mel_all[0, :8], "tm", [(i + 1, i) for i in range(n_tm - 1)])
    windows = whole(
        upsample_kernel,
        shape((16, ROWS, 192), bf16),
        (
            jnp.stack([time_index == 0, time_index == n_tm - 1]).astype(jnp.int32),
            mel_all,
            before,
            after,
            w_full,
            w_here,
        ),
        scratch=[pltpu.VMEM((EXT, MEL_PAD), f32), pltpu.VMEM((1032, 192), f32)],
        cost=cost_of(5 * 10**8, 2 << 20),
        smem=1,
    )
    up_x = exchange(windows)

    flags = jnp.stack([here_index == 0, here_index == n_all - 1]).astype(jnp.int32)
    out = pl.pallas_call(
        conv_kernel,
        out_shape=shape((64, 3072), bf16),
        in_specs=[pl.BlockSpec(memory_space=pltpu.SMEM)] * 2 + vmem_specs(2) + [raw] * 8,
        out_specs=pl.BlockSpec(memory_space=pltpu.VMEM),
        scratch_shapes=[
            pltpu.VMEM((4, ROWS, 768), bf16),
            pltpu.VMEM((4 * STRIDE, 768), bf16),
            pltpu.VMEM((4 * STRIDE, 768), bf16),
            pltpu.VMEM((16, 144, 768), bf16),
            pltpu.VMEM((16, 144, 768), bf16),
            pltpu.SemaphoreType.DMA((2, 4, 4)),
        ],
        compiler_params=pltpu.CompilerParams(vmem_limit_bytes=60 << 20),
        cost_estimate=cost_of(2 * 10**9, 8 << 20, 1 << 18),
        name="convolutions",
    )(
        flags,
        place,
        up_x,
        snake_alpha,
        dil_own,
        dil_core,
        dil_y,
        dil_both,
        plain_own,
        plain_core,
        plain_y,
        plain_both,
    )
    return (mel_next, out.reshape(256, 768))


def solution(mesh):
    in_specs = (
        P(("tm", "sub"), None),
        P(),
        P(None, None, "sub"),
        P("sub", None),
        P(None, "sub"),
        P("sub", None),
        P(),
        P("tm", None),
        P(None, "sub", None),
        P(None, "sub", None),
        P(),
        P(None, "sub", None),
        P(None, "sub", None),
    )
    out_specs = (P("tm", None), P(("tm", "sub"), None))
    return jax.shard_map(program, mesh=mesh, in_specs=in_specs, out_specs=out_specs, check_vma=False)
```

```python
import math

import jax
import jax.numpy as jnp
from jax import lax
from jax.experimental import pallas as pl
from jax.experimental.pallas import tpu as pltpu
from jax.sharding import PartitionSpec as P


HEAD_DIM = 64
BLK = 256
MEL_PAD = 128
OFFSETS = 9

epsilon = 1e-06
bf16 = jnp.bfloat16
f32 = jnp.float32


def norm_rows(rows, offset_row, scale_row):
    rows = rows.astype(f32)
    center = jnp.mean(rows, axis=-1, keepdims=True)
    square = jnp.mean(rows * rows, axis=-1, keepdims=True)
    spread = square - center * center
    return (rows - center) * lax.rsqrt(spread + epsilon) * (1.0 + scale_row) + offset_row


def mm(a, b):
    return jnp.dot(a, b, preferred_element_type=f32)


def mm_t(a, b):
    return lax.dot_general(a, b, (((1,), (1,)), ((), ())), preferred_element_type=f32)


def vmem_specs(n):
    return [pl.BlockSpec(memory_space=pltpu.VMEM)] * n


def whole(kernel, out_shapes, args, scratch=(), cost=None, smem=0, vmem=24):
    single = not isinstance(out_shapes, (tuple, list))
    return pl.pallas_call(
        kernel,
        out_shape=out_shapes,
        in_specs=[pl.BlockSpec(memory_space=pltpu.SMEM)] * smem + vmem_specs(len(args) - smem),
        out_specs=vmem_specs(1)[0] if single else vmem_specs(len(out_shapes)),
        scratch_shapes=list(scratch),
        compiler_params=pltpu.CompilerParams(vmem_limit_bytes=vmem << 20),
        cost_estimate=cost,
    )(*args)


def cost_of(flops, nbytes, trans=0):
    return pl.CostEstimate(flops=flops, bytes_accessed=nbytes, transcendentals=trans)


def first_weights_kernel(
    w_ref, o_ref, pre_ref, dil_ref, plain_ref, a_ref, b_ref, voc_ref, pre_scratch, sems
):
    moves = (
        (w_ref.at[0], a_ref.at[pl.ds(0, 64), :]),
        (w_ref.at[1], a_ref.at[pl.ds(64, 64), :]),
        (w_ref.at[2], b_ref.at[pl.ds(0, 64), :]),
        (o_ref, b_ref.at[pl.ds(64, 64), :]),
        (dil_ref, voc_ref.at[pl.ds(96, 144), :]),
        (plain_ref, voc_ref.at[pl.ds(240, 144), :]),
        (pre_ref, pre_scratch),
    )
    copies = [pltpu.make_async_copy(src, dst, sems.at[n]) for n, (src, dst) in enumerate(moves)]
    for copy in copies:
        copy.start()
    voc_ref[0:96, :] = jnp.zeros((96, 768), bf16)
    copies[6].wait()
    for k in range(7):
        voc_ref[0:96, 100 * k : 100 * k + 100] = pre_scratch[k]
    for copy in copies[:6]:
        copy.wait()


def mlp_weights_kernel(up_ref, down_ref, out_ref):
    out_ref[0:1024, :] = up_ref[...]
    for k in range(4):
        out_ref[1024 + 256 * k : 1280 + 256 * k, :] = down_ref[:, 256 * k : 256 * k + 256]


TAP_ORDER = (2, 3, 4, 5, 6, 7, 0, 1)


def upsample_weights_kernel(w_ref, out_ref):
    for s in range(16):
        for t, tap in enumerate(TAP_ORDER):
            out_ref[s, :, 48 * t : 48 * t + 48] = w_ref[tap, :, 48 * s : 48 * s + 48]


def attention_kernel(flag_ref, mod_ref, *refs):
    row_refs, weight_refs = refs[:8], refs[8:16]
    o0, o1, o2, o3, rows, w_a, w_v, w_out, heads, sems = refs[16:]
    copies = []
    for n, ref in enumerate(row_refs):
        copies.append((ref, rows.at[pl.ds(64 * n, 64), :]))
    for h in range(4):
        first_half, second_half = weight_refs[2 * h], weight_refs[2 * h + 1]
        copies.append((first_half, w_a.at[h]))
        copies.append((second_half.at[pl.ds(0, 64), :], w_v.at[h]))
        copies.append((second_half.at[pl.ds(64, 64), :], w_out.at[pl.ds(64 * h, 64), :]))
    copies = [pltpu.make_async_copy(src, dst, sems.at[n]) for n, (src, dst) in enumerate(copies)]
    for copy in copies:
        copy.start()
    first = flag_ref[0] > 0
    scale = 1.0 / math.sqrt(HEAD_DIM)
    for copy in copies[:8]:
        copy.wait()
    normed = norm_rows(rows[...], mod_ref[0:1, :], mod_ref[1:2, :]).astype(bf16)
    own, back = normed[:BLK], normed[BLK:]
    for copy in copies[8:]:
        copy.wait()

    def one_head(h):
        qk = mm_t(own, w_a[h]).astype(bf16)
        q, k = qk[:, 0:64], qk[:, 64:128]
        v = mm_t(own, w_v[h]).astype(bf16)
        kb = mm_t(back, w_a[h, 64:128, :]).astype(bf16)
        vb = mm_t(back, w_v[h]).astype(bf16)
        s_own = mm_t(q, k) * scale
        s_back = mm_t(q, kb) * scale
        s_back = jnp.where(first, -1e30, s_back)
        top = jnp.maximum(
            jnp.max(s_own, axis=-1, keepdims=True), jnp.max(s_back, axis=-1, keepdims=True)
        )
        e_own = jnp.exp(s_own - top)
        e_back = jnp.exp(s_back - top)
        total = jnp.sum(e_own, axis=-1, keepdims=True) + jnp.sum(e_back, axis=-1, keepdims=True)
        inv = 1.0 / total
        p_own = (e_own * inv).astype(bf16)
        p_back = (e_back * inv).astype(bf16)
        heads[h] = (mm(p_own, v) + mm(p_back, vb)).astype(bf16)

    lax.fori_loop(0, 4, lambda h, c: (one_head(h), c)[1], 0)
    outs = jnp.concatenate([heads[h] for h in range(4)], axis=1)
    total = mm(outs, w_out[...]).astype(bf16)
    for k, out in enumerate((o0, o1, o2, o3)):
        out[...] = total[64 * k : 64 * k + 64]


def sum_of(p0, p1, p2, p3):
    return (p0[...].astype(f32) + p1[...].astype(f32)) + (p2[...].astype(f32) + p3[...].astype(f32))


def after_attention_kernel(p0, p1, p2, p3, frames_ref, mod_ref, mixed_ref, norm_ref):
    attn = sum_of(p0, p1, p2, p3)
    mixed = (frames_ref[...].astype(f32) + mod_ref[2:3, :] * attn).astype(bf16)
    mixed_ref[...] = mixed
    norm_ref[...] = norm_rows(mixed, mod_ref[3:4, :], mod_ref[4:5, :]).astype(bf16)


def mlp_kernel(h0, h1, h2, h3, w0, w1, w2, w3, o0, o1, o2, o3, acc):
    h = jnp.concatenate([h0[...], h1[...], h2[...], h3[...]], axis=0)
    for i, w in enumerate((w0, w1, w2, w3)):
        up = mm(h, w[0:1024, :])
        hid = jax.nn.gelu(up, approximate=True).astype(bf16)
        for k in range(4):
            part = mm(hid, w[1024 + 256 * k : 1280 + 256 * k, :])
            cols = slice(256 * k, 256 * k + 256)
            if i == 0:
                acc[:, cols] = part
            elif i < 3:
                acc[:, cols] += part
            else:
                value = (acc[:, cols] + part).astype(bf16)
                for n, out in enumerate((o0, o1, o2, o3)):
                    out[:, cols] = value[64 * n : 64 * n + 64]


def after_mlp_kernel(p0, p1, p2, p3, mixed_ref, mod_ref, wv_ref, noisy_ref, out_ref):
    feed = sum_of(p0, p1, p2, p3)
    final = (mixed_ref[...].astype(f32) + mod_ref[5:6, :] * feed).astype(bf16)
    normed = norm_rows(final, mod_ref[6:7, :], mod_ref[7:8, :]).astype(bf16)
    mel = noisy_ref[...] + 0.5 * mm(normed, wv_ref[...])
    for s in range(16):
        out_ref[s] = mel


def placed_kernel(comp_ref, full_ref, here_ref):
    earlier = lax.broadcasted_iota(jnp.int32, (100, 192), 1) < 96
    full_ref[...] = jnp.zeros(full_ref.shape, bf16)
    here_ref[...] = jnp.zeros(here_ref.shape, bf16)
    here = [comp_ref[100 * j : 100 * j + 100, 0:192] for j in range(7)]
    near = [comp_ref[100 * j : 100 * j + 100, 192:384] for j in range(7)]
    for d in range(OFFSETS):
        value = jnp.zeros((100, 192), f32)
        if 0 <= d - 1 < 7:
            value = here[d - 1]
            here_ref[MEL_PAD * d : MEL_PAD * d + 100, :] = value.astype(bf16)
        if d < 7:
            value = value + jnp.where(earlier, near[d], 0.0)
        if 0 <= d - 2 < 7:
            value = value + jnp.where(earlier, 0.0, near[d - 2])
        full_ref[MEL_PAD * d : MEL_PAD * d + 100, :] = value.astype(bf16)


EXT = 1056


def upsample_kernel(flag_ref, mel_ref, before_ref, after_ref, full_ref, here_ref, out_ref, ext, up):
    ext[...] = jnp.zeros((EXT, MEL_PAD), f32)
    ext[0:8, 0:100] = before_ref[...]
    for s in range(16):
        ext[8 + 64 * s : 72 + 64 * s, 0:100] = mel_ref[s]
    ext[1032:1040, 0:100] = after_ref[...]
    cols = [ext[3 + k : 3 + k + 1032, :].astype(bf16) for k in range(OFFSETS)]
    up[...] = mm(jnp.concatenate(cols, axis=1), full_ref[...])
    earlier = lax.broadcasted_iota(jnp.int32, (8, 192), 1) < 96
    row = lax.broadcasted_iota(jnp.int32, (8, 192), 0)
    for which, base, r in ((0, 0, 1), (1, 1024, 0)):
        edge_cols = [ext[base + 3 + k : base + 11 + k, :].astype(bf16) for k in range(OFFSETS)]
        edge = mm(jnp.concatenate(edge_cols, axis=1), here_ref[...])
        lanes = earlier if which == 0 else jnp.logical_not(earlier)
        use = (flag_ref[which] > 0) & (row == r) & lanes
        up[base : base + 8, :] = jnp.where(use, edge, up[base : base + 8, :])
    for s in range(16):
        out_ref[s] = up[64 * s : 64 * s + ROWS, :].astype(bf16)


PI_PARTS = (3.140625, 0.000965118408203125, 2.5331974029541016e-06, 1.984187258941006e-09)


def sin_squared(x):
    k = jnp.round(x * (1.0 / math.pi))
    r = x
    for part in PI_PARTS:
        r = r - k * part
    z = r * r
    poly = -2.3889859e-08 * z + 2.7525562e-06
    poly = poly * z - 1.9840874e-04
    poly = poly * z + 8.3333310e-03
    poly = poly * z - 1.6666667e-01
    sine = r + r * (z * poly)
    return sine * sine


def snake_act(values, alpha_row, inverse_row):
    return values + sin_squared(alpha_row * values) * inverse_row


def shifted(plane, by):
    return pltpu.roll(plane, by % plane.shape[0], 0)


ROWS = 72


X_STEPS = (0, 3, 1, 2)


def shard_of(place_ref, which, step):
    return ((place_ref[0] + X_STEPS[step]) & 3) * 4 + (place_ref[1] ^ which)


def merge_kernel(own, left, right, far_top, far_bottom, pre_ref, dil_ref, plain_ref, sems):
    moves = []
    for n, ref in enumerate((own, left, right)):
        moves.append((ref.at[pl.ds(0, 96), :], pre_ref.at[n]))
        moves.append((ref.at[pl.ds(96, 144), :], dil_ref.at[n]))
        moves.append((ref.at[pl.ds(240, 144), :], plain_ref.at[n]))
    moves.append((far_top.at[pl.ds(0, 96), :], pre_ref.at[3]))
    moves.append((far_top.at[pl.ds(96, 144), :], dil_ref.at[3]))
    moves.append((far_bottom, plain_ref.at[3]))
    copies = [pltpu.make_async_copy(src, dst, sems.at[n]) for n, (src, dst) in enumerate(moves)]
    for copy in copies:
        copy.start()
    for copy in copies:
        copy.wait()


def prelude_weights_kernel(place_ref, p0, p1, p2, p3, out_ref, sems):
    copies = [
        pltpu.make_async_copy(
            ref.at[step], out_ref.at[shard_of(place_ref, which, step)], sems.at[which, step]
        )
        for which, ref in enumerate((p0, p1, p2, p3))
        for step in range(4)
    ]
    for copy in copies:
        copy.start()
    for copy in copies:
        copy.wait()


STRIDE = 80


def conv_kernel(flag_ref, place_ref, up_ref, alpha_ref, *refs):
    out_ref, planes, act_one, act_two, w_one, w_two, sems = refs[8:]
    copies = [
        [
            pltpu.make_async_copy(
                refs[4 * k + which].at[step],
                buf.at[shard_of(place_ref, which, step)],
                sems.at[k, which, step],
            )
            for which in range(4)
            for step in range(4)
        ]
        for k, buf in enumerate((w_one, w_two))
    ]
    for half in copies:
        for copy in half:
            copy.start()
    first = flag_ref[0] > 0
    last = flag_ref[1] > 0
    row = lax.broadcasted_iota(jnp.int32, (ROWS, 256), 0)
    outside = (first & (row == 0)) | (last & (row == 65))

    def gather_channels(g, carry):
        lanes = pl.ds(pl.multiple_of(384 * g, 384), 384)
        for p in range(4):
            parts = [up_ref[8 * g + i, :, 48 * p : 48 * p + 48] for i in range(8)]
            planes[p, :, lanes] = jnp.concatenate(parts, axis=1)
        return carry

    lax.fori_loop(0, 2, gather_channels, 0)
    act_one[...] = jnp.zeros(act_one.shape, bf16)
    act_two[...] = jnp.zeros(act_two.shape, bf16)

    def columns(n):
        return pl.ds(pl.multiple_of(256 * n, 256), 256)

    def up_plane(p, cols):
        return jnp.where(outside, 0.0, planes[p, :, cols].astype(f32))

    def products(act_ref, w_ref, cols):
        act = act_ref[...]
        y = []
        for tap in range(3):
            weight = jnp.concatenate(
                [w_ref[s, 48 * tap : 48 * tap + 48, cols] for s in range(16)], axis=0
            )
            v = mm(act, weight)
            y.append([v[STRIDE * p : STRIDE * p + ROWS] for p in range(4)])
        return y

    def first_act(n, carry):
        cols = columns(n)
        alpha = alpha_ref[0:1, cols]
        for p in range(4):
            value = snake_act(up_plane(p, cols), alpha, 1.0 / alpha).astype(bf16)
            act_one[STRIDE * p : STRIDE * p + ROWS, cols] = value
        return carry

    def first_conv(n, carry):
        cols = columns(n)
        alpha = alpha_ref[1:2, cols]
        y = products(act_one, w_one, cols)
        for p in range(4):
            before = y[0][0] if p == 3 else shifted(y[0][p + 1], 1)
            after = y[2][3] if p == 0 else shifted(y[2][p - 1], -1)
            value = snake_act(before + y[1][p] + after, alpha, 1.0 / alpha)
            value = jnp.where(outside, 0.0, value).astype(bf16)
            act_two[STRIDE * p : STRIDE * p + ROWS, cols] = value
        return carry

    def second_conv(n, carry):
        cols = columns(n)
        y = products(act_two, w_two, cols)
        for p in range(4):
            before = y[0][p - 1] if p >= 1 else shifted(y[0][3], 1)
            after = y[2][p + 1] if p <= 2 else shifted(y[2][0], -1)
            total = up_plane(p, cols) + (before + y[1][p] + after)
            to = pl.ds(pl.multiple_of(768 * p + 256 * n, 256), 256)
            out_ref[:, to] = shifted(total, -1)[0:64].astype(bf16)
        return carry

    lax.fori_loop(0, 3, first_act, 0)
    for copy in copies[0]:
        copy.wait()
    lax.fori_loop(0, 3, first_conv, 0)
    for copy in copies[1]:
        copy.wait()
    lax.fori_loop(0, 3, second_conv, 0)


def exchange(value, groups=None, axis="sub"):
    return lax.all_to_all(value, axis, 0, 0, tiled=True, axis_index_groups=groups)


def device(y_hi, z, x, y_lo, core):
    return (y_hi * 8 + z) * 16 + x * 4 + y_lo * 2 + core


OTHER_Y = [
    (device(h, z, x, y, c), device(1 - h, z, x, 1 - y, c))
    for h in range(2)
    for z in range(8)
    for x in range(4)
    for y in range(2)
    for c in range(2)
]
OTHER_GROUPS = [
    [device(y ^ side, z, x, y, c) for x in range(4) for y in range(2) for c in range(2)]
    for side in range(2)
    for z in range(8)
]


def program(
    frames,
    modulation,
    w_project,
    w_heads_out,
    w_up,
    w_down,
    w_velocity,
    noisy_mel,
    w_prelude,
    w_upsample,
    snake_alpha,
    w_dilated,
    w_plain,
):
    own_rows = frames.shape[0]
    sub_index = lax.axis_index("sub")
    time_index = lax.axis_index("tm")
    n_sub = lax.axis_size("sub")
    n_tm = lax.axis_size("tm")
    n_all = n_sub * n_tm
    both = ("tm", "sub")
    shape = jax.ShapeDtypeStruct
    here_index = time_index * n_sub + sub_index

    to_right = [(i, (i + 4) % 16) for i in range(16)]
    to_left = [(i, (i - 4) % 16) for i in range(16)]
    own_a, own_b, w_voc = pl.pallas_call(
        first_weights_kernel,
        out_shape=(shape((128, 1024), bf16), shape((128, 1024), bf16), shape((384, 768), bf16)),
        in_specs=[pl.BlockSpec(memory_space=pl.ANY)] * 5,
        out_specs=vmem_specs(3),
        scratch_shapes=[pltpu.VMEM((7, 96, 100), bf16), pltpu.SemaphoreType.DMA((7,))],
        compiler_params=pltpu.CompilerParams(vmem_limit_bytes=60 << 20),
        cost_estimate=cost_of(0, 3 << 20),
        name="first_weights",
    )(
        jnp.swapaxes(w_project, 1, 2),
        w_heads_out,
        w_prelude,
        w_dilated.reshape(144, 768),
        w_plain.reshape(144, 768),
    )
    back_frames = lax.ppermute(frames, both, [(i, i + 4) for i in range(n_all - 4)])
    left_a = lax.ppermute(own_a, "sub", to_right)
    right_b = lax.ppermute(own_b, "sub", to_left)
    left_b = lax.ppermute(own_b, "sub", to_right)
    right_a = lax.ppermute(own_a, "sub", to_left)
    far_a = lax.ppermute(left_a, "sub", to_right)
    far_b = lax.ppermute(right_b, "sub", to_left)

    voc_left = lax.ppermute(w_voc, "sub", to_right)
    voc_right = lax.ppermute(w_voc, "sub", to_left)
    voc_top = lax.ppermute(voc_left[:240], "sub", to_right)
    voc_bottom = lax.ppermute(voc_right[240:], "sub", to_left)
    pre_shape, conv_shape = shape((4, 96, 768), bf16), shape((4, 144, 768), bf16)
    raw = pl.BlockSpec(memory_space=pl.ANY)
    pre_own, dil_own, plain_own = pl.pallas_call(
        merge_kernel,
        out_shape=(pre_shape, conv_shape, conv_shape),
        in_specs=[raw] * 5,
        out_specs=vmem_specs(3),
        scratch_shapes=[pltpu.SemaphoreType.DMA((12,))],
        compiler_params=pltpu.CompilerParams(vmem_limit_bytes=60 << 20),
        cost_estimate=cost_of(0, 5 << 20),
        name="voc_merge",
    )(w_voc, voc_left, voc_right, voc_top, voc_bottom)
    beside = [[(i, i ^ k) for i in range(16)] for k in (1, 2, 3)]
    pre_y = lax.ppermute(pre_own, both, OTHER_Y)
    dil_y = lax.ppermute(dil_own, both, OTHER_Y)
    plain_y = lax.ppermute(plain_own, "sub", beside[1])
    pre_core = lax.ppermute(pre_own, "sub", beside[0])
    dil_core = lax.ppermute(dil_own, "sub", beside[0])
    plain_core = lax.ppermute(plain_own, "sub", beside[0])
    pre_both = lax.ppermute(pre_y, "sub", beside[0])
    dil_both = lax.ppermute(dil_y, "sub", beside[0])
    plain_both = lax.ppermute(plain_y, "sub", beside[0])
    place = jnp.stack([sub_index // 4, lax.rem(sub_index, 4)]).astype(jnp.int32)

    block = [frames] + [lax.ppermute(frames, "sub", beside[k - 1]) for k in (1, 2, 3)]
    back = [back_frames] + [lax.ppermute(back_frames, "sub", beside[k - 1]) for k in (1, 2, 3)]

    own_mlp = whole(
        mlp_weights_kernel, shape((2048, 256), bf16), (w_up, w_down), cost=cost_of(0, 2 << 20)
    )
    other_core = lax.ppermute(own_mlp, "sub", [(i, i ^ 1) for i in range(16)])
    other_y = lax.ppermute(own_mlp, both, OTHER_Y)
    other_both = lax.ppermute(other_y, "sub", [(i, i ^ 1) for i in range(16)])

    ups = whole(
        upsample_weights_kernel, shape((16, 96, 384), bf16), (w_upsample,), cost=cost_of(0, 3 << 20)
    )

    is_first = (time_index == 0) & (sub_index < 4)
    quarter = shape((own_rows, 1024), bf16)
    partial = pl.pallas_call(
        attention_kernel,
        out_shape=(quarter,) * 4,
        in_specs=[pl.BlockSpec(memory_space=pltpu.SMEM)]
        + vmem_specs(1)
        + [pl.BlockSpec(memory_space=pl.ANY)] * 16,
        out_specs=vmem_specs(4),
        scratch_shapes=[
            pltpu.VMEM((2 * BLK, 1024), bf16),
            pltpu.VMEM((4, 128, 1024), bf16),
            pltpu.VMEM((4, 64, 1024), bf16),
            pltpu.VMEM((256, 1024), bf16),
            pltpu.VMEM((4, BLK, 64), bf16),
            pltpu.SemaphoreType.DMA((20,)),
        ],
        compiler_params=pltpu.CompilerParams(vmem_limit_bytes=60 << 20),
        cost_estimate=cost_of(10**9, 4 << 20, 1 << 19),
        name="attention",
    )(
        is_first.astype(jnp.int32).reshape(1),
        modulation,
        *block,
        *back,
        own_a,
        own_b,
        left_a,
        left_b,
        right_a,
        right_b,
        far_a,
        far_b,
    )
    ups = exchange(ups, OTHER_GROUPS, both)
    parts = [partial[0]] + [lax.ppermute(partial[k], "sub", beside[k - 1]) for k in (1, 2, 3)]
    mixed_rows, own_norm = whole(
        after_attention_kernel,
        (quarter, quarter),
        (*parts, frames, modulation),
        cost=cost_of(10**6, 1 << 20),
    )

    own_norm, ups = lax.optimization_barrier((own_norm, ups))
    across = [(i, (i + 8) % 16) for i in range(16)]
    second = [
        own_norm,
        lax.ppermute(own_norm, "sub", across),
        lax.ppermute(own_norm, "sub", to_right),
        lax.ppermute(own_norm, "sub", to_left),
    ]
    partial = whole(
        mlp_kernel,
        (quarter,) * 4,
        (*second, own_mlp, other_core, other_y, other_both),
        scratch=[pltpu.VMEM((256, 1024), f32)],
        cost=cost_of(11 * 10**8, 5 << 20, 1 << 18),
    )
    parts = [
        partial[0],
        lax.ppermute(partial[1], "sub", across),
        lax.ppermute(partial[2], "sub", to_left),
        lax.ppermute(partial[3], "sub", to_right),
    ]
    noisy_own = lax.dynamic_slice_in_dim(noisy_mel, sub_index * own_rows, own_rows, 0)
    copies = whole(
        after_mlp_kernel,
        shape((16, own_rows, 100), f32),
        (*parts, mixed_rows, modulation, w_velocity, noisy_own),
        cost=cost_of(10**7, 1 << 20),
    )
    mel_all = exchange(copies)
    mel_next = mel_all.reshape(-1, 100)

    pre_all = pl.pallas_call(
        prelude_weights_kernel,
        out_shape=shape((16, 96, 768), bf16),
        in_specs=[pl.BlockSpec(memory_space=pltpu.SMEM)] + [raw] * 4,
        out_specs=pl.BlockSpec(memory_space=pltpu.VMEM),
        scratch_shapes=[pltpu.SemaphoreType.DMA((4, 4))],
        compiler_params=pltpu.CompilerParams(vmem_limit_bytes=60 << 20),
        cost_estimate=cost_of(0, 5 << 20),
        name="prelude_weights",
    )(place, pre_own, pre_core, pre_y, pre_both).reshape(1536, 768)
    comp = lax.dot_general(
        pre_all, ups.reshape(1536, 384), (((0,), (0,)), ((), ())), preferred_element_type=f32
    )
    w_full, w_here = whole(
        placed_kernel,
        (shape((OFFSETS * MEL_PAD, 192), bf16), shape((OFFSETS * MEL_PAD, 192), bf16)),
        (comp,),
        cost=cost_of(10**6, 2 << 20),
    )

    before = lax.ppermute(mel_all[15, 56:], "tm", [(i, i + 1) for i in range(n_tm - 1)])
    after = lax.ppermute(mel_all[0, :8], "tm", [(i + 1, i) for i in range(n_tm - 1)])
    windows = whole(
        upsample_kernel,
        shape((16, ROWS, 192), bf16),
        (
            jnp.stack([time_index == 0, time_index == n_tm - 1]).astype(jnp.int32),
            mel_all,
            before,
            after,
            w_full,
            w_here,
        ),
        scratch=[pltpu.VMEM((EXT, MEL_PAD), f32), pltpu.VMEM((1032, 192), f32)],
        cost=cost_of(5 * 10**8, 2 << 20),
        smem=1,
    )
    up_x = exchange(windows)

    flags = jnp.stack([here_index == 0, here_index == n_all - 1]).astype(jnp.int32)
    out = pl.pallas_call(
        conv_kernel,
        out_shape=shape((64, 3072), bf16),
        in_specs=[pl.BlockSpec(memory_space=pltpu.SMEM)] * 2 + vmem_specs(2) + [raw] * 8,
        out_specs=pl.BlockSpec(memory_space=pltpu.VMEM),
        scratch_shapes=[
            pltpu.VMEM((4, ROWS, 768), bf16),
            pltpu.VMEM((4 * STRIDE, 768), bf16),
            pltpu.VMEM((4 * STRIDE, 768), bf16),
            pltpu.VMEM((16, 144, 768), bf16),
            pltpu.VMEM((16, 144, 768), bf16),
            pltpu.SemaphoreType.DMA((2, 4, 4)),
        ],
        compiler_params=pltpu.CompilerParams(vmem_limit_bytes=60 << 20),
        cost_estimate=cost_of(2 * 10**9, 8 << 20, 1 << 18),
        name="convolutions",
    )(
        flags,
        place,
        up_x,
        snake_alpha,
        dil_own,
        dil_core,
        dil_y,
        dil_both,
        plain_own,
        plain_core,
        plain_y,
        plain_both,
    )
    return (mel_next, out.reshape(256, 768))


def solution(mesh):
    in_specs = (
        P(("tm", "sub"), None),
        P(),
        P(None, None, "sub"),
        P("sub", None),
        P(None, "sub"),
        P("sub", None),
        P(),
        P("tm", None),
        P(None, "sub", None),
        P(None, "sub", None),
        P(),
        P(None, "sub", None),
        P(None, "sub", None),
    )
    out_specs = (P("tm", None), P(("tm", "sub"), None))
    return jax.shard_map(program, mesh=mesh, in_specs=in_specs, out_specs=out_specs, check_vma=False)
```
